256 devices in a mesh: seq: 64 (over z, y, core), head: 4 (over x).
Axes of the slice: x: 4, y: 4, z: 8, core: 2. Of those that a mesh axis runs over, the one named last changes fastest.
Arguments:
- queries: bfloat16 [49152, 4096], P(('seq', 'head')), may hold values from -6 to 6
- key_rows: bfloat16 [49152, 4096], P(('seq', 'head')), may hold values from -6 to 6
- values: bfloat16 [49152, 4096], P(('seq', 'head')), may hold values from -6 to 6
- doc_ids: int32 [49152], replicated, may hold values from 0 to 127, as said below
- image_flags: int32 [49152], replicated, may hold values from 0 to 1, as said below
- labels: int32 [49152], P(('seq', 'head')), may hold values from -1 to 31999, as said below
- token_loss: float32 [49152], P(('seq', 'head')), may hold values from 0.05 to 8
Outputs:
- attended: bfloat16 [49152, 4096], P(('seq', 'head'))
- doc_count: float32 [128], replicated
- doc_loss: float32 [128], replicated
The draws below stay inside these ranges and needn't reach their ends.
Inputs may be any that keep to these rules, and one draw needn't show every extreme that they name: `doc_ids`: document numbers never fall along the sequence and rise by one from one document to the next; every document holds at least 64 and at most 704 tokens, and some document holds exactly 704. `image_flags`: the 1s form spans of exactly 576 consecutive tokens, at most one span a document, each inside one document and never at its first token. `labels`: every image token has -1, and some document has -1 on all of its tokens.
All inputs are finite; a program needn't handle non-finite values.
Results may differ from the reference program's by a relative error of at most 0.0034.
Values may be sent and summed in bfloat16 or wider, within the bound.
A program may use at most 128 MiB of HBM per device.

```python
import math
import jax
import jax.numpy as jnp
from jax import lax

HEADS = 32
HEAD_DIM = 128
VOCAB = 32000
TOK_DEV = 768
DOC_MEAN = 384
DOC_MOST = 704
IMG_LEN = 576
TOKENS = 49152
DOCS = 128
N_SEQ = 64


def layout(key):
    base = jax.random.fold_in(key, 7001)
    spare = (DOC_MOST - DOC_MEAN) // 2
    ratio = TOK_DEV // DOC_MEAN
    offsets = jax.random.randint(jax.random.fold_in(base, 1), (DOCS + 1,), -spare, spare + 1).astype(jnp.int32)
    offsets = offsets.at[0].set(0).at[DOCS].set(0)
    lowest = max(1, IMG_LEN + 1 - DOC_MEAN - spare)
    reach = jax.random.randint(jax.random.fold_in(base, 2), (N_SEQ - 1,), lowest, spare + 1).astype(jnp.int32)
    picked = jax.random.randint(jax.random.fold_in(base, 3), (), 0, N_SEQ - 1)
    reach = reach.at[picked].set(spare)
    block_index = jnp.arange(1, N_SEQ, dtype=jnp.int32)
    boundary_doc = block_index * ratio
    offsets = offsets.at[boundary_doc - 1].set(-spare)
    offsets = offsets.at[boundary_doc].set(reach)
    bounds = (jnp.arange(DOCS + 1, dtype=jnp.int32) * DOC_MEAN + offsets).astype(jnp.int32)
    starts = bounds[:-1]
    ends = bounds[1:]
    lengths = ends - starts
    places = jnp.arange(TOKENS, dtype=jnp.int32)
    docs = jnp.searchsorted(ends, places, side='right').astype(jnp.int32)
    room = lengths - IMG_LEN
    offset = 1 + jax.random.randint(jax.random.fold_in(base, 4), (DOCS,), 0, jnp.maximum(room, 1))
    chosen = (jax.random.randint(jax.random.fold_in(base, 5), (DOCS,), 0, 2) == 1) & (room >= 1)
    image_start = (starts + offset).astype(jnp.int32)
    image_start = image_start.at[boundary_doc - 1].set(block_index * TOK_DEV + reach - IMG_LEN)
    chosen = chosen.at[boundary_doc - 1].set(True)
    flags = chosen[docs] & (places >= image_start[docs]) & (places < image_start[docs] + IMG_LEN)
    return (docs, flags.astype(jnp.int32))


def draw_doc_ids(key, part):
    return layout(key)[0]


def draw_image_flags(key, part):
    return layout(key)[1]


def draw_labels(key, part):
    docs, flags = layout(key)
    token_ids = jax.random.randint(jax.random.fold_in(key, 7101), (TOKENS,), 0, VOCAB)
    dropped = jax.random.randint(jax.random.fold_in(key, 7102), (TOKENS,), 0, 8) == 0
    silent = jax.random.randint(jax.random.fold_in(key, 7103), (2,), 0, DOCS)
    muted = (docs == silent[0]) | (docs == silent[1])
    return jnp.where((flags == 1) | dropped | muted, -1, token_ids).astype(jnp.int32)


def draw_queries(key, part):
    columns = HEADS * HEAD_DIM
    field = jnp.clip(jax.random.normal(jax.random.fold_in(key, 7303), (TOKENS, columns), jnp.float32), -5.0, 5.0)
    return field.astype(jnp.bfloat16)


def draw_key_rows(key, part):
    columns = HEADS * HEAD_DIM
    field = jnp.clip(jax.random.normal(jax.random.fold_in(key, 7403), (TOKENS, columns), jnp.float32), -5.0, 5.0)
    return field.astype(jnp.bfloat16)


def block_scale(own_key, dims, split, least, high):
    def one(dim, parts):
        heights = jax.random.uniform(jax.random.fold_in(jax.random.fold_in(own_key, 6), dim), (parts,), jnp.float32, least / len(split), high / len(split))
        return jnp.repeat(jnp.exp(heights), dims[dim] // parts).reshape((-1,) + (1,) * (len(dims) - dim - 1))

    level = one(*split[0])
    for cut in split[1:]:
        level = level * one(*cut)
    return level


def noise(key, extent, deviation, most, split=(), kind=jnp.bfloat16):
    result = deviation * jax.random.normal(key, extent, jnp.float32)
    if split:
        result = result * block_scale(key, extent, split, -0.22, 0.18)
    return jnp.clip(result, -most, most).astype(kind)


def setup_inputs(seed: int = 0) -> dict:
    arg_keys = jax.random.split(jax.random.key(seed), 8)
    return {
        "queries": draw_queries(jax.random.fold_in(arg_keys[7], 71), 0),
        "key_rows": draw_key_rows(jax.random.fold_in(arg_keys[7], 71), 0),
        "values": noise(arg_keys[2], (TOKENS, HEADS * HEAD_DIM), 1.0, 6.0, ((0, 256),)),
        "doc_ids": draw_doc_ids(jax.random.fold_in(arg_keys[7], 71), 0),
        "image_flags": draw_image_flags(jax.random.fold_in(arg_keys[7], 71), 0),
        "labels": draw_labels(jax.random.fold_in(arg_keys[7], 71), 0),
        "token_loss": jnp.clip(jnp.exp(math.log(8.0) - 5.075174 * jax.random.uniform(arg_keys[6], (TOKENS,), jnp.float32) ** block_scale(arg_keys[6], (TOKENS,), ((0, 256),), -0.2, 0.2)), 0.05, 8.0),
    }


def allowed_pairs(query_docs, query_flags, query_places, key_docs, key_flags, key_places):
    same = query_docs[:, None] == key_docs[None, :]
    earlier = key_places[None, :] <= query_places[:, None]
    image = (query_flags[:, None] == 1) & (key_flags[None, :] == 1)
    return same & (earlier | image)


def attend(query_part, key_window, value_window, allowed):
    outputs = []
    scale = HEAD_DIM ** -0.5
    for head_index in range(query_part.shape[1] // HEAD_DIM):
        lower = head_index * HEAD_DIM
        query_head = query_part[:, lower:lower + HEAD_DIM]
        key_head = key_window[:, lower:lower + HEAD_DIM]
        value_head = value_window[:, lower:lower + HEAD_DIM]
        scores = lax.dot_general(query_head, key_head, (((1,), (1,)), ((), ())), preferred_element_type=jnp.float32) * scale
        scores = jnp.where(allowed, scores, -jnp.inf)
        row_max = jnp.max(scores, axis=1, keepdims=True)
        weights = jnp.exp(scores - row_max)
        total = jnp.sum(weights, axis=1, keepdims=True)
        mixed = jnp.dot(weights.astype(jnp.bfloat16), value_head, preferred_element_type=jnp.float32) / total
        outputs.append(mixed.astype(jnp.bfloat16))
    return jnp.concatenate(outputs, axis=1)


def reference(queries, key_rows, values, doc_ids, image_flags, labels, token_loss):
    reach_back = (DOC_MOST + TOK_DEV - 2) // TOK_DEV
    reach_front = (IMG_LEN + TOK_DEV - 2) // TOK_DEV
    window = (reach_back + 1 + reach_front) * TOK_DEV

    def one_block(index):
        query_start = index * TOK_DEV
        key_start = jnp.clip(query_start - reach_back * TOK_DEV, 0, TOKENS - window).astype(jnp.int32)
        query_part = lax.dynamic_slice_in_dim(queries, query_start, TOK_DEV, 0)
        key_window = lax.dynamic_slice_in_dim(key_rows, key_start, window, 0)
        value_window = lax.dynamic_slice_in_dim(values, key_start, window, 0)
        query_docs = lax.dynamic_slice_in_dim(doc_ids, query_start, TOK_DEV, 0)
        query_flags = lax.dynamic_slice_in_dim(image_flags, query_start, TOK_DEV, 0)
        key_docs = lax.dynamic_slice_in_dim(doc_ids, key_start, window, 0)
        key_flags = lax.dynamic_slice_in_dim(image_flags, key_start, window, 0)
        query_places = query_start + jnp.arange(TOK_DEV, dtype=jnp.int32)
        key_places = key_start + jnp.arange(window, dtype=jnp.int32)
        allowed = allowed_pairs(query_docs, query_flags, query_places, key_docs, key_flags, key_places)
        return attend(query_part, key_window, value_window, allowed)

    blocks = lax.map(one_block, jnp.arange(N_SEQ, dtype=jnp.int32))
    attended = blocks.reshape(TOKENS, queries.shape[1])
    documents = TOKENS // DOC_MEAN
    member = (doc_ids[:, None] == jnp.arange(documents, dtype=jnp.int32)[None, :]) & (labels[:, None] >= 0)
    doc_count = jnp.sum(member.astype(jnp.float32), axis=0)
    loss_sum = jnp.sum(jnp.where(member, token_loss[:, None], jnp.float32(0.0)), axis=0)
    doc_loss = loss_sum / jnp.maximum(doc_count, jnp.float32(1.0))
    return attended, doc_count, doc_loss
```

```python
import functools
import math

import jax
import jax.numpy as jnp
from jax import lax
from jax.experimental import pallas as pl
from jax.experimental.pallas import tpu as pltpu
from jax.sharding import Mesh
from jax.sharding import PartitionSpec as P

HEAD_DIM = 128
DOC_MEAN = 384
NZ, NY, NC, NX = 8, 4, 2, 4
GROUP = NC * NX
STRIP = 192
BLOCK = STRIP * GROUP
BLOCKS = NZ * NY
HEADS = 4
BACK, AHEAD = 704, 576
FRONT = 768
SPAN = 1536
WINDOW = FRONT + BLOCK + 640
DEPTH = 3
LANES = 128
AXES = ("z", "y", "c", "x")
MESH = pl.DeviceIdType.MESH


def first_key(strip):
    return pl.multiple_of(((3 * strip + 1) // 2) * LANES, LANES)


def kernel(
    q_hbm,
    k_hbm,
    v_hbm,
    docs_hbm,
    flags_hbm,
    stat_ref,
    out_hbm,
    count_ref,
    loss_ref,
    q_buf,
    k_buf,
    v_buf,
    o_buf,
    bias,
    docs,
    flags,
    q_docs,
    q_images,
    slots_a,
    slots_b,
    slots_c,
    id_sem,
    in_send,
    in_recv,
    halo_send,
    halo_recv,
    out_send,
    out_recv,
    stat_send,
    stat_recv,
):
    z, y, c, x = (lax.axis_index(name) for name in AXES)
    me = c * NX + x
    block = z * NY + y
    after = lax.rem(block + 1, BLOCKS)
    before = lax.rem(block + BLOCKS - 1, BLOCKS)

    def member(index):
        return {"z": z, "y": y, "c": lax.div(index, NX), "x": lax.rem(index, NX)}

    def in_block(index):
        return {"z": lax.div(index, NY), "y": lax.rem(index, NY), "c": c, "x": x}

    def along_y(index):
        return {"z": z, "y": index, "c": c, "x": x}

    def along_z(index):
        return {"z": index, "y": y, "c": c, "x": x}

    id_copies = [
        pltpu.make_async_copy(docs_hbm, docs, id_sem.at[0]),
        pltpu.make_async_copy(flags_hbm, flags, id_sem.at[1]),
    ]
    for copy in id_copies:
        copy.start()

    barrier = pltpu.get_barrier_semaphore()
    peers = [member(lax.rem(me + o, GROUP)) for o in range(1, GROUP)]
    peers += [in_block(after), in_block(before)]
    peers += [along_y(lax.rem(y + o, NY)) for o in range(1, NY)]
    peers += [along_z(lax.rem(z + o, NZ)) for o in range(1, NZ)]
    for peer in peers:
        pl.semaphore_signal(barrier, inc=1, device_id=peer, device_id_type=MESH)
    pl.semaphore_wait(barrier, len(peers))

    sources = (k_hbm, v_hbm, q_hbm)
    targets = (k_buf, v_buf, q_buf)
    bases = (FRONT, FRONT, 0)

    def piece(array, head, owner):
        columns = pl.ds(pl.multiple_of(owner * HEADS * HEAD_DIM + head * HEAD_DIM, LANES), HEAD_DIM)
        rows = pl.ds(pl.multiple_of(bases[array] + me * STRIP, 64), STRIP)
        return sources[array].at[:, columns], targets[array].at[head, rows, :]

    def start_group(group):
        array, head = divmod(group, HEADS)

        def send(o, carry):
            owner = lax.rem(me + o, GROUP)
            source, target = piece(array, head, owner)
            pltpu.make_async_remote_copy(
                src_ref=source,
                dst_ref=target,
                send_sem=in_send.at[array],
                recv_sem=in_recv.at[array, head],
                device_id=member(owner),
                device_id_type=MESH,
            ).start()
            return carry

        lax.fori_loop(1, GROUP, send, 0)
        source, target = piece(array, head, me)
        pltpu.make_async_copy(source, target, in_recv.at[array, head]).start()

    def wait_group(group):
        array, head = divmod(group, HEADS)
        rows = targets[array].at[head, pl.ds(bases[array], BLOCK), :]
        pltpu.make_async_copy(rows, rows, in_recv.at[array, head]).wait()

    def start_halo(array, head):
        buffer = targets[array]
        for rows, first, target, peer in (
            (BACK, FRONT + BLOCK - BACK, FRONT - BACK, after),
            (AHEAD, FRONT, FRONT + BLOCK, before),
        ):
            pltpu.make_async_remote_copy(
                src_ref=buffer.at[head, pl.ds(first, rows), :],
                dst_ref=buffer.at[head, pl.ds(target, rows), :],
                send_sem=halo_send.at[array],
                recv_sem=halo_recv.at[array, head],
                device_id=in_block(peer),
                device_id_type=MESH,
            ).start()

    def stage_send(number, slots, own, size, peer_of):
        def send(o, carry):
            pltpu.make_async_remote_copy(
                src_ref=slots.at[own],
                dst_ref=slots.at[own],
                send_sem=stat_send.at[number],
                recv_sem=stat_recv.at[number],
                device_id=peer_of(lax.rem(own + o, size)),
                device_id_type=MESH,
            ).start()
            return carry

        lax.fori_loop(1, size, send, 0)

    def stage_sum(number, slots, size):
        others = slots.at[pl.ds(0, size - 1)]
        pltpu.make_async_copy(others, others, stat_recv.at[number]).wait()
        total = slots[0]
        for i in range(1, size):
            total = total + slots[i]
        return total

    def after_groups(group):
        if group == 0:
            for copy in id_copies:
                copy.wait()
            make_query_ids()
        elif group == 1:
            total = stage_sum(0, slots_a, GROUP)
            slots_b[y] = total
            stage_send(1, slots_b, y, NY, along_y)
        elif group == 3:
            total = stage_sum(1, slots_b, NY)
            slots_c[z] = total
            stage_send(2, slots_c, z, NZ, along_z)
        elif group == 5:
            total = stage_sum(2, slots_c, NZ)
            counts = total[0:1]
            count_ref[...] = counts
            loss_ref[...] = total[1:2] / jnp.maximum(counts, 1.0)

    def id_row(row):
        at = pl.ds(lax.rem(block * (BLOCK // LANES) + row + BLOCKS * (BLOCK // LANES), BLOCKS * (BLOCK // LANES)), 1)
        doc = docs[at, :]
        return doc, jnp.where(flags[at, :] == 1, doc, -1)

    def make_query_ids():
        def one(row, carry):
            at = pl.ds(pl.multiple_of(row * LANES, LANES), LANES)
            doc, image = id_row(row)
            q_docs[at, :] = jnp.broadcast_to(doc, (LANES, LANES)).T
            q_images[at, :] = jnp.broadcast_to(image, (LANES, LANES)).T
            return carry

        lax.fori_loop(0, BLOCK // LANES, one, 0)

    def make_bias(strip):
        start = first_key(strip)
        rows = pl.ds(pl.multiple_of(strip * STRIP, 64), STRIP)
        doc, image = q_docs[rows, :], q_images[rows, :]
        shape = (STRIP, LANES)
        offset = lax.broadcasted_iota(jnp.int32, shape, 1) - lax.broadcasted_iota(jnp.int32, shape, 0)
        first_row = lax.div(start, LANES) - FRONT // LANES
        for i in range(SPAN // LANES):
            key_doc, key_image = id_row(first_row + i)
            key_image = jnp.where(key_image < 0, -2, key_image)
            earlier = offset <= FRONT + strip * STRIP - start - i * LANES
            allowed = ((doc == key_doc) & earlier) | (image == key_image)
            bias[rows, i * LANES : (i + 1) * LANES] = jnp.where(allowed, 0.0, -jnp.inf)

    def attend(head, strip):
        start = first_key(strip)
        rows = pl.ds(pl.multiple_of(strip * STRIP, 64), STRIP)
        keys = pl.ds(start, SPAN)
        scores = lax.dot_general(
            q_buf[head, rows, :],
            k_buf[head, keys, :],
            (((1,), (1,)), ((), ())),
            preferred_element_type=jnp.float32,
        )
        scores = scores * (HEAD_DIM**-0.5 * math.log2(math.e)) + bias[rows, :]
        weights = jnp.exp2(scores - jnp.max(scores, axis=1, keepdims=True))
        total = jnp.sum(weights, axis=1, keepdims=True)
        mixed = jnp.dot(
            weights.astype(jnp.bfloat16), v_buf[head, keys, :], preferred_element_type=jnp.float32
        )
        o_buf[head, rows, :] = (mixed / total).astype(jnp.bfloat16)
        columns = pl.ds(pl.multiple_of(me * HEADS * HEAD_DIM + head * HEAD_DIM, LANES), HEAD_DIM)
        source, target = o_buf.at[head, rows, :], out_hbm.at[:, columns]

        @pl.when(strip == me)
        def _():
            pltpu.make_async_copy(source, target, out_recv).start()

        @pl.when(strip != me)
        def _():
            pltpu.make_async_remote_copy(
                src_ref=source,
                dst_ref=target,
                send_sem=out_send,
                recv_sem=out_recv,
                device_id=member(strip),
                device_id_type=MESH,
            ).start()

    for group in range(DEPTH):
        start_group(group)
    slots_a[me] = stat_ref[...]
    stage_send(0, slots_a, me, GROUP, member)

    edge = jnp.zeros((HEADS, 64, HEAD_DIM), jnp.bfloat16)
    for buffer in (k_buf, v_buf):
        buffer[:, 0 : FRONT - BACK, :] = edge
        buffer[:, FRONT + BLOCK + AHEAD : WINDOW, :] = edge

    for group in range(2 * HEADS):
        wait_group(group)
        start_halo(*divmod(group, HEADS))
        start_group(group + DEPTH)
        after_groups(group)
        make_bias(group)

    for head in range(HEADS):
        for array in range(2):
            rows = targets[array].at[head, pl.ds(0, BACK + AHEAD), :]
            pltpu.make_async_copy(rows, rows, halo_recv.at[array, head]).wait()
        group = 2 * HEADS + head
        wait_group(group)
        if group + DEPTH < 3 * HEADS:
            start_group(group + DEPTH)

        def step(i, carry, head=head):
            attend(head, lax.rem(me + i, GROUP))
            return carry

        lax.fori_loop(1, GROUP + 1, step, 0)

    def drain(ref, sem):
        pltpu.make_async_copy(ref, ref, sem).wait()

    for array in range(3):
        drain(targets[array].at[:, pl.ds(0, BLOCK - STRIP), :], in_send.at[array])
    for array in range(2):
        drain(targets[array].at[:, pl.ds(0, BACK + AHEAD), :], halo_send.at[array])
    for number, slots, size in ((0, slots_a, GROUP), (1, slots_b, NY), (2, slots_c, NZ)):
        drain(slots.at[pl.ds(0, size - 1)], stat_send.at[number])
    drain(o_buf.at[:, pl.ds(0, BLOCK - STRIP), :], out_send)
    drain(out_hbm, out_recv)


def per_device(queries, key_rows, values, doc_ids, image_flags, labels, token_loss):
    rows = labels.shape[0]
    place = ((lax.axis_index("z") * NY + lax.axis_index("y")) * NC + lax.axis_index("c")) * NX + lax.axis_index("x")
    local_docs = lax.dynamic_slice_in_dim(doc_ids, place * rows, rows)
    documents = doc_ids.shape[0] // DOC_MEAN
    member = (local_docs[:, None] == jnp.arange(documents, dtype=jnp.int32)[None, :]) & (labels[:, None] >= 0)
    counts = jnp.sum(member.astype(jnp.float32), axis=0)
    sums = jnp.sum(jnp.where(member, token_loss[:, None], jnp.float32(0.0)), axis=0)
    stats = jnp.pad(jnp.stack([counts, sums]), ((0, 6), (0, 0)))
    id_shape = (BLOCKS * BLOCK // LANES, LANES)
    anywhere = pl.BlockSpec(memory_space=pl.ANY)
    local = pl.BlockSpec(memory_space=pltpu.VMEM)
    window = pltpu.VMEM((HEADS, WINDOW, HEAD_DIM), jnp.bfloat16)
    own = pltpu.VMEM((HEADS, BLOCK, HEAD_DIM), jnp.bfloat16)
    attended, counts, losses = pl.pallas_call(
        kernel,
        name="exchange_and_attend",
        out_shape=(
            jax.ShapeDtypeStruct(queries.shape, jnp.bfloat16),
            jax.ShapeDtypeStruct((1, LANES), jnp.float32),
            jax.ShapeDtypeStruct((1, LANES), jnp.float32),
        ),
        in_specs=[anywhere] * 5 + [local],
        out_specs=(anywhere, local, local),
        scratch_shapes=[
            own,
            window,
            window,
            own,
            pltpu.VMEM((BLOCK, SPAN), jnp.float32),
            pltpu.VMEM(id_shape, jnp.int32),
            pltpu.VMEM(id_shape, jnp.int32),
            pltpu.VMEM((BLOCK, LANES), jnp.int32),
            pltpu.VMEM((BLOCK, LANES), jnp.int32),
            pltpu.VMEM((GROUP, 8, LANES), jnp.float32),
            pltpu.VMEM((NY, 8, LANES), jnp.float32),
            pltpu.VMEM((NZ, 8, LANES), jnp.float32),
            pltpu.SemaphoreType.DMA((2,)),
            pltpu.SemaphoreType.DMA((3,)),
            pltpu.SemaphoreType.DMA((3, HEADS)),
            pltpu.SemaphoreType.DMA((2,)),
            pltpu.SemaphoreType.DMA((2, HEADS)),
            pltpu.SemaphoreType.DMA,
            pltpu.SemaphoreType.DMA,
            pltpu.SemaphoreType.DMA((3,)),
            pltpu.SemaphoreType.DMA((3,)),
        ],
        compiler_params=pltpu.CompilerParams(
            collective_id=0, has_side_effects=True, vmem_limit_bytes=56 * 1024 * 1024
        ),
    )(queries, key_rows, values, doc_ids.reshape(id_shape), image_flags.reshape(id_shape), stats)
    return attended, counts.reshape(documents), losses.reshape(documents)


def solution(mesh):
    split = Mesh(mesh.devices.reshape(NZ, NY, NC, NX), AXES)
    return jax.shard_map(
        per_device,
        mesh=split,
        in_specs=(
            P(AXES, None),
            P(AXES, None),
            P(AXES, None),
            P(),
            P(),
            P(AXES),
            P(AXES),
        ),
        out_specs=(P(AXES, None), P(), P()),
        check_vma=False,
    )
```

```python
import functools
import math

import jax
import jax.numpy as jnp
from jax import lax
from jax.experimental import pallas as pl
from jax.experimental.pallas import tpu as pltpu
from jax.sharding import Mesh
from jax.sharding import PartitionSpec as P

HEAD_DIM = 128
DOC_MEAN = 384
NZ, NY, NC, NX = 8, 4, 2, 4
GROUP = NC * NX
STRIP = 192
BLOCK = STRIP * GROUP
BLOCKS = NZ * NY
HEADS = 4
BACK, AHEAD = 704, 576
FRONT = 768
SPAN = 1536
WINDOW = FRONT + BLOCK + 640
DEPTH = 3
LANES = 128
AXES = ("z", "y", "c", "x")
MESH = pl.DeviceIdType.MESH


def first_key(strip):
    return pl.multiple_of(((3 * strip + 1) // 2) * LANES, LANES)


def kernel(
    q_hbm,
    k_hbm,
    v_hbm,
    docs_hbm,
    flags_hbm,
    labels_hbm,
    token_loss_hbm,
    out_ref,
    count_ref,
    loss_ref,
    q_buf,
    k_buf,
    v_buf,
    o_buf,
    bias,
    docs,
    flags,
    q_docs,
    q_images,
    slots_a,
    slots_b,
    slots_c,
    labels,
    token_loss,
    id_sem,
    in_send,
    in_recv,
    back_send,
    back_recv,
    ahead_send,
    ahead_recv,
    out_send,
    out_recv,
    stat_send,
    stat_recv,
    relay_send,
    relay_recv,
):
    z, y, c, x = (lax.axis_index(name) for name in AXES)
    me = c * NX + x
    block = z * NY + y
    has_after, has_before = block < BLOCKS - 1, block > 0
    after = lax.rem(block + 1, BLOCKS)
    before = lax.rem(block + BLOCKS - 1, BLOCKS)
    has_upper, has_lower = z < NZ - 1, z > 0
    upper, lower = lax.rem(z + 1, NZ), lax.rem(z + NZ - 1, NZ)

    def member(index):
        return {"z": z, "y": y, "c": lax.div(index, NX), "x": lax.rem(index, NX)}

    def in_block(index):
        return {"z": lax.div(index, NY), "y": lax.rem(index, NY), "c": c, "x": x}

    def along_y(index):
        return {"z": z, "y": index, "c": c, "x": x}

    def along_z(index):
        return {"z": index, "y": y, "c": c, "x": x}

    id_copies = [
        pltpu.make_async_copy(docs_hbm, docs, id_sem.at[0]),
        pltpu.make_async_copy(flags_hbm, flags, id_sem.at[1]),
        pltpu.make_async_copy(labels_hbm, labels, id_sem.at[2]),
        pltpu.make_async_copy(token_loss_hbm, token_loss, id_sem.at[3]),
    ]
    for copy in id_copies:
        copy.start()

    barrier = pltpu.get_barrier_semaphore()
    peers = [member(lax.rem(me + o, GROUP)) for o in range(1, GROUP)]
    peers += [along_y(lax.rem(y + o, NY)) for o in range(1, NY)]
    for peer in peers:
        pl.semaphore_signal(barrier, inc=1, device_id=peer, device_id_type=MESH)
    expected = len(peers)
    for present, peer in (
        (has_after, in_block(after)),
        (has_before, in_block(before)),
        (has_upper, along_z(upper)),
        (has_lower, along_z(lower)),
    ):
        expected = expected + present.astype(jnp.int32)

        @pl.when(present)
        def _(peer=peer):
            pl.semaphore_signal(barrier, inc=1, device_id=peer, device_id_type=MESH)

    pl.semaphore_wait(barrier, expected)

    def drain(ref, sem):
        pltpu.make_async_copy(ref, ref, sem).wait()

    sources = (k_hbm, v_hbm, q_hbm)
    targets = (k_buf, v_buf, q_buf)
    bases = (FRONT, FRONT, 0)

    def piece(array, head, owner):
        columns = pl.ds(pl.multiple_of(owner * HEADS * HEAD_DIM + head * HEAD_DIM, LANES), HEAD_DIM)
        rows = pl.ds(pl.multiple_of(bases[array] + me * STRIP, 64), STRIP)
        return sources[array].at[:, columns], targets[array].at[head, rows, :]

    def start_group(group):
        array, head = divmod(group, HEADS)

        def send(o, carry):
            owner = lax.rem(me + o, GROUP)
            source, target = piece(array, head, owner)
            pltpu.make_async_remote_copy(
                src_ref=source,
                dst_ref=target,
                send_sem=in_send.at[array],
                recv_sem=in_recv.at[array, head],
                device_id=member(owner),
                device_id_type=MESH,
            ).start()
            return carry

        lax.fori_loop(1, GROUP, send, 0)
        source, target = piece(array, head, me)
        pltpu.make_async_copy(source, target, in_recv.at[array, head]).start()

    def wait_group(group):
        array, head = divmod(group, HEADS)
        rows = targets[array].at[head, pl.ds(bases[array], BLOCK), :]
        pltpu.make_async_copy(rows, rows, in_recv.at[array, head]).wait()

    def halos(array, head):
        return (
            (has_after, has_before, BACK, FRONT + BLOCK - BACK, FRONT - BACK, after, back_send, back_recv),
            (has_before, has_after, AHEAD, FRONT, FRONT + BLOCK, before, ahead_send, ahead_recv),
        )

    def start_halo(array, head):
        buffer = targets[array]
        for sends, _, rows, first, target, peer, send_sem, recv_sem in halos(array, head):

            @pl.when(sends)
            def _():
                pltpu.make_async_remote_copy(
                    src_ref=buffer.at[head, pl.ds(first, rows), :],
                    dst_ref=buffer.at[head, pl.ds(target, rows), :],
                    send_sem=send_sem.at[array],
                    recv_sem=recv_sem.at[array, head],
                    device_id=in_block(peer),
                    device_id_type=MESH,
                ).start()

    def wait_halo(array, head):
        for _, receives, rows, _, target, _, _, recv_sem in halos(array, head):

            @pl.when(receives)
            def _():
                drain(targets[array].at[head, pl.ds(target, rows), :], recv_sem.at[array, head])

    def drain_halo(array):
        for sends, _, rows, _, _, _, send_sem, _ in halos(array, 0):

            @pl.when(sends)
            def _():
                drain(targets[array].at[:, pl.ds(0, rows), :], send_sem.at[array])

    def stage_send(number, slots, own, size, peer_of):
        def send(o, carry):
            pltpu.make_async_remote_copy(
                src_ref=slots.at[own],
                dst_ref=slots.at[own],
                send_sem=stat_send.at[number],
                recv_sem=stat_recv.at[number],
                device_id=peer_of(lax.rem(own + o, size)),
                device_id_type=MESH,
            ).start()
            return carry

        lax.fori_loop(1, size, send, 0)

    def stage_sum(number, slots, size):
        others = slots.at[pl.ds(0, size - 1)]
        pltpu.make_async_copy(others, others, stat_recv.at[number]).wait()
        total = slots[0]
        for i in range(1, size):
            total = total + slots[i]
        return total

    def relays(step):
        return (
            (has_upper & (z >= step), z - step, has_lower & (z >= step + 1), z - 1 - step, upper, 0),
            (has_lower & (z + step < NZ), z + step, has_upper & (z + step + 1 < NZ), z + 1 + step, lower, 1),
        )

    def relay_copy(step, slot, peer, way):
        return pltpu.make_async_remote_copy(
            src_ref=slots_c.at[slot],
            dst_ref=slots_c.at[slot],
            send_sem=relay_send.at[way, step],
            recv_sem=relay_recv.at[way, step],
            device_id=along_z(peer),
            device_id_type=MESH,
        )

    def relay_start(step):
        for sends, slot, _, _, peer, way in relays(step):

            @pl.when(sends)
            def _():
                relay_copy(step, slot, peer, way).start()

    def relay_wait(step):
        for _, _, receives, slot, peer, way in relays(step):

            @pl.when(receives)
            def _():
                drain(slots_c.at[slot], relay_recv.at[way, step])

    def relay_drain(step):
        for sends, slot, _, _, peer, way in relays(step):

            @pl.when(sends)
            def _():
                drain(slots_c.at[slot], relay_send.at[way, step])

    def document_partials():
        first = lax.div(block * BLOCK + me * STRIP, LANES)
        pair = jnp.concatenate([docs[pl.ds(first, 1), :], docs[pl.ds(first + 1, 1), :]], axis=1)
        half = jnp.concatenate([pair[:, 64:], pair[:, :64]], axis=1)
        doc = jnp.where(lax.rem(me, 2) == 1, half, pair)[:, :STRIP]
        weight = jnp.where(labels[...] >= 0, 1.0, 0.0)
        lines = lax.broadcasted_iota(jnp.int32, (8, STRIP), 0)
        terms = jnp.where(lines == 0, weight, jnp.where(lines == 1, weight * token_loss[...], 0.0))
        hit = jnp.where(lax.broadcasted_iota(jnp.int32, (LANES, STRIP), 0) == doc, 1.0, 0.0)
        return lax.dot_general(
            terms,
            hit,
            (((1,), (1,)), ((), ())),
            precision=lax.Precision.HIGHEST,
            preferred_element_type=jnp.float32,
        )

    def totals_step(point):
        if point == 0:
            for copy in id_copies:
                copy.wait()
            slots_a[me] = document_partials()
            stage_send(0, slots_a, me, GROUP, member)
            make_query_ids()
        elif point == 1:
            slots_b[y] = stage_sum(0, slots_a, GROUP)
            stage_send(1, slots_b, y, NY, along_y)
        elif point == 2:
            slots_c[z] = stage_sum(1, slots_b, NY)
            relay_start(0)
        else:
            relay_wait(point - 3)
            if point - 2 < NZ - 1:
                relay_start(point - 2)
            else:
                total = slots_c[0]
                for i in range(1, NZ):
                    total = total + slots_c[i]
                counts = total[0:1]
                count_ref[...] = counts
                loss_ref[...] = total[1:2] / jnp.maximum(counts, 1.0)

    def id_row(row):
        at = pl.ds(lax.rem(block * (BLOCK // LANES) + row + BLOCKS * (BLOCK // LANES), BLOCKS * (BLOCK // LANES)), 1)
        doc = docs[at, :]
        return doc, jnp.where(flags[at, :] == 1, doc, -1)

    def make_query_ids():
        def one(row, carry):
            at = pl.ds(pl.multiple_of(row * LANES, LANES), LANES)
            doc, image = id_row(row)
            q_docs[at, :] = jnp.broadcast_to(doc, (LANES, LANES)).T
            q_images[at, :] = jnp.broadcast_to(image, (LANES, LANES)).T
            return carry

        lax.fori_loop(0, BLOCK // LANES, one, 0)

    def make_bias(strip):
        start = first_key(strip)
        rows = pl.ds(pl.multiple_of(strip * STRIP, 64), STRIP)
        doc, image = q_docs[rows, :], q_images[rows, :]
        shape = (STRIP, LANES)
        offset = lax.broadcasted_iota(jnp.int32, shape, 1) - lax.broadcasted_iota(jnp.int32, shape, 0)
        first_row = lax.div(start, LANES) - FRONT // LANES
        for i in range(SPAN // LANES):
            key_doc, key_image = id_row(first_row + i)
            key_image = jnp.where(key_image < 0, -2, key_image)
            earlier = offset <= FRONT + strip * STRIP - start - i * LANES
            allowed = ((doc == key_doc) & earlier) | (image == key_image)
            bias[rows, i * LANES : (i + 1) * LANES] = jnp.where(allowed, 0.0, -jnp.inf)

    def attend(head, strip):
        start = first_key(strip)
        rows = pl.ds(pl.multiple_of(strip * STRIP, 64), STRIP)
        keys = pl.ds(start, SPAN)
        scores = lax.dot_general(
            q_buf[head, rows, :],
            k_buf[head, keys, :],
            (((1,), (1,)), ((), ())),
            preferred_element_type=jnp.float32,
        )
        scores = scores * (HEAD_DIM**-0.5 * math.log2(math.e)) + bias[rows, :]
        weights = jnp.exp2(scores - jnp.max(scores, axis=1, keepdims=True))
        total = jnp.sum(weights, axis=1, keepdims=True)
        mixed = jnp.dot(
            weights.astype(jnp.bfloat16), v_buf[head, keys, :], preferred_element_type=jnp.float32
        )
        o_buf[head, rows, :] = (mixed / total).astype(jnp.bfloat16)
        columns = pl.ds(pl.multiple_of(me * HEADS * HEAD_DIM + head * HEAD_DIM, LANES), HEAD_DIM)
        source, target = o_buf.at[head, rows, :], out_ref.at[:, columns]

        @pl.when(strip == me)
        def _():
            pltpu.make_async_copy(source, target, out_recv).start()

        @pl.when(strip != me)
        def _():
            pltpu.make_async_remote_copy(
                src_ref=source,
                dst_ref=target,
                send_sem=out_send,
                recv_sem=out_recv,
                device_id=member(strip),
                device_id_type=MESH,
            ).start()

    for group in range(DEPTH):
        start_group(group)

    edge = jnp.zeros((HEADS, 64, HEAD_DIM), jnp.bfloat16)
    for buffer in (k_buf, v_buf):
        buffer[:, 0 : FRONT - BACK, :] = edge
        buffer[:, FRONT + BLOCK + AHEAD : WINDOW, :] = edge

    @pl.when(block == 0)
    def _():
        for buffer in (k_buf, v_buf):
            buffer[:, FRONT - BACK : FRONT, :] = jnp.zeros((HEADS, BACK, HEAD_DIM), jnp.bfloat16)

    @pl.when(block == BLOCKS - 1)
    def _():
        for buffer in (k_buf, v_buf):
            buffer[:, FRONT + BLOCK : FRONT + BLOCK + AHEAD, :] = jnp.zeros((HEADS, AHEAD, HEAD_DIM), jnp.bfloat16)

    for group in range(2 * HEADS):
        wait_group(group)
        start_halo(*divmod(group, HEADS))
        start_group(group + DEPTH)
        totals_step(group)
        make_bias(group)

    for head in range(HEADS):
        for array in range(2):
            wait_halo(array, head)
        group = 2 * HEADS + head
        wait_group(group)
        if group + DEPTH < 3 * HEADS:
            start_group(group + DEPTH)

        def step(i, carry, head=head):
            attend(head, lax.rem(me + i, GROUP))
            return carry

        lax.fori_loop(1, GROUP + 1, step, 0)
        if head < 2:
            totals_step(2 * HEADS + head)

    for array in range(3):
        drain(targets[array].at[:, pl.ds(0, BLOCK - STRIP), :], in_send.at[array])
    for array in range(2):
        drain_halo(array)
    for number, slots, size in ((0, slots_a, GROUP), (1, slots_b, NY)):
        drain(slots.at[pl.ds(0, size - 1)], stat_send.at[number])
    for number in range(NZ - 1):
        relay_drain(number)
    drain(o_buf.at[:, pl.ds(0, BLOCK - STRIP), :], out_send)
    drain(out_ref, out_recv)


def per_device(queries, key_rows, values, doc_ids, image_flags, labels, token_loss):
    documents = doc_ids.shape[0] // DOC_MEAN
    id_shape = (BLOCKS * BLOCK // LANES, LANES)
    anywhere = pl.BlockSpec(memory_space=pl.ANY)
    local = pl.BlockSpec(memory_space=pltpu.VMEM)
    window = pltpu.VMEM((HEADS, WINDOW, HEAD_DIM), jnp.bfloat16)
    own = pltpu.VMEM((HEADS, BLOCK, HEAD_DIM), jnp.bfloat16)
    attended, counts, losses = pl.pallas_call(
        kernel,
        name="exchange_and_attend",
        out_shape=(
            pltpu.VMEM(queries.shape, jnp.bfloat16),
            pltpu.VMEM((1, LANES), jnp.float32),
            pltpu.VMEM((1, LANES), jnp.float32),
        ),
        in_specs=[anywhere] * 7,
        out_specs=(local, local, local),
        scratch_shapes=[
            own,
            window,
            window,
            own,
            pltpu.VMEM((BLOCK, SPAN), jnp.float32),
            pltpu.VMEM(id_shape, jnp.int32),
            pltpu.VMEM(id_shape, jnp.int32),
            pltpu.VMEM((BLOCK, LANES), jnp.int32),
            pltpu.VMEM((BLOCK, LANES), jnp.int32),
            pltpu.VMEM((GROUP, 8, LANES), jnp.float32),
            pltpu.VMEM((NY, 8, LANES), jnp.float32),
            pltpu.VMEM((NZ, 8, LANES), jnp.float32),
            pltpu.VMEM((1, STRIP), jnp.int32),
            pltpu.VMEM((1, STRIP), jnp.float32),
            pltpu.SemaphoreType.DMA((4,)),
            pltpu.SemaphoreType.DMA((3,)),
            pltpu.SemaphoreType.DMA((3, HEADS)),
            pltpu.SemaphoreType.DMA((2,)),
            pltpu.SemaphoreType.DMA((2, HEADS)),
            pltpu.SemaphoreType.DMA((2,)),
            pltpu.SemaphoreType.DMA((2, HEADS)),
            pltpu.SemaphoreType.DMA,
            pltpu.SemaphoreType.DMA,
            pltpu.SemaphoreType.DMA((2,)),
            pltpu.SemaphoreType.DMA((2,)),
            pltpu.SemaphoreType.DMA((2, NZ - 1)),
            pltpu.SemaphoreType.DMA((2, NZ - 1)),
        ],
        compiler_params=pltpu.CompilerParams(
            collective_id=0, has_side_effects=True, vmem_limit_bytes=40 * 1024 * 1024
        ),
    )(
        *(
            pltpu.with_memory_space_constraint(array, pltpu.HBM)
            for array in (
                queries,
                key_rows,
                values,
                doc_ids.reshape(id_shape),
                image_flags.reshape(id_shape),
                labels.reshape(1, STRIP),
                token_loss.reshape(1, STRIP),
            )
        )
    )
    return attended, counts.reshape(documents), losses.reshape(documents)


def solution(mesh):
    split = Mesh(mesh.devices.reshape(NZ, NY, NC, NX), AXES)
    return jax.shard_map(
        per_device,
        mesh=split,
        in_specs=(
            P(AXES, None),
            P(AXES, None),
            P(AXES, None),
            P(),
            P(),
            P(AXES),
            P(AXES),
        ),
        out_specs=(P(AXES, None), P(), P()),
        check_vma=False,
    )
```

```python
import functools
import math

import jax
import jax.numpy as jnp
from jax import lax
from jax.experimental import pallas as pl
from jax.experimental.pallas import tpu as pltpu
from jax.sharding import Mesh
from jax.sharding import PartitionSpec as P

HEAD_DIM = 128
DOC_MEAN = 384
NZ, NY, NC, NX = 8, 4, 2, 4
GROUP = NC * NX
STRIP = 192
BLOCK = STRIP * GROUP
BLOCKS = NZ * NY
HEADS = 4
BACK, AHEAD = 704, 576
FRONT = 768
SPAN = 1536
WINDOW = FRONT + BLOCK + 640
DEPTH = 3
LANES = 128
AXES = ("z", "y", "c", "x")
MESH = pl.DeviceIdType.MESH


def first_key(strip):
    return pl.multiple_of(((3 * strip + 1) // 2) * LANES, LANES)


def kernel(
    q_hbm,
    k_hbm,
    v_hbm,
    docs_hbm,
    flags_hbm,
    labels_hbm,
    token_loss_hbm,
    out_ref,
    count_ref,
    loss_ref,
    q_buf,
    k_buf,
    v_buf,
    o_buf,
    bias,
    docs,
    flags,
    q_docs,
    q_images,
    slots_a,
    slots_b,
    slots_c,
    labels,
    token_loss,
    id_sem,
    in_send,
    in_recv,
    back_send,
    back_recv,
    ahead_send,
    ahead_recv,
    out_send,
    out_recv,
    stat_send,
    stat_recv,
    relay_send,
    relay_recv,
):
    z, y, c, x = (lax.axis_index(name) for name in AXES)
    me = c * NX + x
    block = z * NY + y
    has_after, has_before = block < BLOCKS - 1, block > 0
    after = lax.rem(block + 1, BLOCKS)
    before = lax.rem(block + BLOCKS - 1, BLOCKS)
    has_upper, has_lower = z < NZ - 1, z > 0
    upper, lower = lax.rem(z + 1, NZ), lax.rem(z + NZ - 1, NZ)

    def member(index):
        return {"z": z, "y": y, "c": lax.div(index, NX), "x": lax.rem(index, NX)}

    def in_block(index):
        return {"z": lax.div(index, NY), "y": lax.rem(index, NY), "c": c, "x": x}

    def along_y(index):
        return {"z": z, "y": index, "c": c, "x": x}

    def along_z(index):
        return {"z": index, "y": y, "c": c, "x": x}

    id_copies = [
        pltpu.make_async_copy(docs_hbm, docs, id_sem.at[0]),
        pltpu.make_async_copy(flags_hbm, flags, id_sem.at[1]),
        pltpu.make_async_copy(labels_hbm, labels, id_sem.at[2]),
        pltpu.make_async_copy(token_loss_hbm, token_loss, id_sem.at[3]),
    ]
    for copy in id_copies:
        copy.start()

    barrier = pltpu.get_barrier_semaphore()
    peers = [member(lax.rem(me + o, GROUP)) for o in range(1, GROUP)]
    peers += [along_y(lax.rem(y + o, NY)) for o in range(1, NY)]
    for peer in peers:
        pl.semaphore_signal(barrier, inc=1, device_id=peer, device_id_type=MESH)
    expected = len(peers)
    for present, peer in (
        (has_after, in_block(after)),
        (has_before, in_block(before)),
        (has_upper, along_z(upper)),
        (has_lower, along_z(lower)),
    ):
        expected = expected + present.astype(jnp.int32)

        @pl.when(present)
        def _(peer=peer):
            pl.semaphore_signal(barrier, inc=1, device_id=peer, device_id_type=MESH)

    pl.semaphore_wait(barrier, expected)

    def drain(ref, sem):
        pltpu.make_async_copy(ref, ref, sem).wait()

    sources = (k_hbm, v_hbm, q_hbm)
    targets = (k_buf, v_buf, q_buf)
    bases = (FRONT, FRONT, 0)

    def piece(array, head, owner):
        columns = pl.ds(pl.multiple_of(owner * HEADS * HEAD_DIM + head * HEAD_DIM, LANES), HEAD_DIM)
        rows = pl.ds(pl.multiple_of(bases[array] + me * STRIP, 64), STRIP)
        return sources[array].at[:, columns], targets[array].at[head, rows, :]

    def start_group(group):
        array, head = divmod(group, HEADS)

        def send(o, carry):
            owner = lax.rem(me + o, GROUP)
            source, target = piece(array, head, owner)
            pltpu.make_async_remote_copy(
                src_ref=source,
                dst_ref=target,
                send_sem=in_send.at[array],
                recv_sem=in_recv.at[array, head],
                device_id=member(owner),
                device_id_type=MESH,
            ).start()
            return carry

        lax.fori_loop(1, GROUP, send, 0)
        source, target = piece(array, head, me)
        pltpu.make_async_copy(source, target, in_recv.at[array, head]).start()

    def wait_group(group):
        array, head = divmod(group, HEADS)
        rows = targets[array].at[head, pl.ds(bases[array], BLOCK), :]
        pltpu.make_async_copy(rows, rows, in_recv.at[array, head]).wait()

    def halos(array, head):
        return (
            (has_after, has_before, BACK, FRONT + BLOCK - BACK, FRONT - BACK, after, back_send, back_recv),
            (has_before, has_after, AHEAD, FRONT, FRONT + BLOCK, before, ahead_send, ahead_recv),
        )

    def start_halo(array, head):
        buffer = targets[array]
        for sends, _, rows, first, target, peer, send_sem, recv_sem in halos(array, head):

            @pl.when(sends)
            def _():
                pltpu.make_async_remote_copy(
                    src_ref=buffer.at[head, pl.ds(first, rows), :],
                    dst_ref=buffer.at[head, pl.ds(target, rows), :],
                    send_sem=send_sem.at[array],
                    recv_sem=recv_sem.at[array, head],
                    device_id=in_block(peer),
                    device_id_type=MESH,
                ).start()

    def wait_halo(array, head):
        for _, receives, rows, _, target, _, _, recv_sem in halos(array, head):

            @pl.when(receives)
            def _():
                drain(targets[array].at[head, pl.ds(target, rows), :], recv_sem.at[array, head])

    def drain_halo(array):
        for sends, _, rows, _, _, _, send_sem, _ in halos(array, 0):

            @pl.when(sends)
            def _():
                drain(targets[array].at[:, pl.ds(0, rows), :], send_sem.at[array])

    def stage_send(number, slots, own, size, peer_of):
        def send(o, carry):
            pltpu.make_async_remote_copy(
                src_ref=slots.at[own],
                dst_ref=slots.at[own],
                send_sem=stat_send.at[number],
                recv_sem=stat_recv.at[number],
                device_id=peer_of(lax.rem(own + o, size)),
                device_id_type=MESH,
            ).start()
            return carry

        lax.fori_loop(1, size, send, 0)

    def stage_sum(number, slots, size):
        others = slots.at[pl.ds(0, size - 1)]
        pltpu.make_async_copy(others, others, stat_recv.at[number]).wait()
        total = slots[0]
        for i in range(1, size):
            total = total + slots[i]
        return total

    def relays(step):
        return (
            (has_upper & (z >= step), z - step, has_lower & (z >= step + 1), z - 1 - step, upper, 0),
            (has_lower & (z + step < NZ), z + step, has_upper & (z + step + 1 < NZ), z + 1 + step, lower, 1),
        )

    def relay_copy(step, slot, peer, way):
        return pltpu.make_async_remote_copy(
            src_ref=slots_c.at[slot],
            dst_ref=slots_c.at[slot],
            send_sem=relay_send.at[way, step],
            recv_sem=relay_recv.at[way, step],
            device_id=along_z(peer),
            device_id_type=MESH,
        )

    def relay_start(step):
        for sends, slot, _, _, peer, way in relays(step):

            @pl.when(sends)
            def _():
                relay_copy(step, slot, peer, way).start()

    def relay_wait(step):
        for _, _, receives, slot, peer, way in relays(step):

            @pl.when(receives)
            def _():
                drain(slots_c.at[slot], relay_recv.at[way, step])

    def relay_drain(step):
        for sends, slot, _, _, peer, way in relays(step):

            @pl.when(sends)
            def _():
                drain(slots_c.at[slot], relay_send.at[way, step])

    def document_partials():
        first = lax.div(block * BLOCK + me * STRIP, LANES)
        pair = jnp.concatenate([docs[pl.ds(first, 1), :], docs[pl.ds(first + 1, 1), :]], axis=1)
        half = jnp.concatenate([pair[:, 64:], pair[:, :64]], axis=1)
        doc = jnp.where(lax.rem(me, 2) == 1, half, pair)[:, :STRIP]
        weight = jnp.where(labels[...] >= 0, 1.0, 0.0)
        lines = lax.broadcasted_iota(jnp.int32, (8, STRIP), 0)
        terms = jnp.where(lines == 0, weight, jnp.where(lines == 1, weight * token_loss[...], 0.0))
        hit = jnp.where(lax.broadcasted_iota(jnp.int32, (LANES, STRIP), 0) == doc, 1.0, 0.0)
        return lax.dot_general(
            terms,
            hit,
            (((1,), (1,)), ((), ())),
            precision=lax.Precision.HIGHEST,
            preferred_element_type=jnp.float32,
        )

    def totals_step(point):
        if point == 0:
            for copy in id_copies:
                copy.wait()
            slots_a[me] = document_partials()
            stage_send(0, slots_a, me, GROUP, member)
            make_query_ids()
        elif point == 1:
            slots_b[y] = stage_sum(0, slots_a, GROUP)
            stage_send(1, slots_b, y, NY, along_y)
        elif point == 2:
            slots_c[z] = stage_sum(1, slots_b, NY)
            relay_start(0)
        else:
            relay_wait(point - 3)
            if point - 2 < NZ - 1:
                relay_start(point - 2)
            else:
                total = slots_c[0]
                for i in range(1, NZ):
                    total = total + slots_c[i]
                counts = total[0:1]
                count_ref[...] = counts
                loss_ref[...] = total[1:2] / jnp.maximum(counts, 1.0)

    def id_row(row):
        at = pl.ds(lax.rem(block * (BLOCK // LANES) + row + BLOCKS * (BLOCK // LANES), BLOCKS * (BLOCK // LANES)), 1)
        doc = docs[at, :]
        return doc, jnp.where(flags[at, :] == 1, doc, -1)

    def make_query_ids():
        def one(row, carry):
            at = pl.ds(pl.multiple_of(row * LANES, LANES), LANES)
            doc, image = id_row(row)
            q_docs[at, :] = jnp.broadcast_to(doc, (LANES, LANES)).T
            q_images[at, :] = jnp.broadcast_to(image, (LANES, LANES)).T
            return carry

        lax.fori_loop(0, BLOCK // LANES, one, 0)

    def make_bias(strip):
        start = first_key(strip)
        rows = pl.ds(pl.multiple_of(strip * STRIP, 64), STRIP)
        doc, image = q_docs[rows, :], q_images[rows, :]
        shape = (STRIP, LANES)
        offset = lax.broadcasted_iota(jnp.int32, shape, 1) - lax.broadcasted_iota(jnp.int32, shape, 0)
        first_row = lax.div(start, LANES) - FRONT // LANES
        for i in range(SPAN // LANES):
            key_doc, key_image = id_row(first_row + i)
            key_image = jnp.where(key_image < 0, -2, key_image)
            earlier = offset <= FRONT + strip * STRIP - start - i * LANES
            allowed = ((doc == key_doc) & earlier) | (image == key_image)
            bias[rows, i * LANES : (i + 1) * LANES] = jnp.where(allowed, 0.0, -jnp.inf)

    def attend(head, strip):
        start = first_key(strip)
        rows = pl.ds(pl.multiple_of(strip * STRIP, 64), STRIP)
        keys = pl.ds(start, SPAN)
        scores = lax.dot_general(
            q_buf[head, rows, :],
            k_buf[head, keys, :],
            (((1,), (1,)), ((), ())),
            preferred_element_type=jnp.float32,
        )
        scores = scores * (HEAD_DIM**-0.5 * math.log2(math.e)) + bias[rows, :]
        weights = jnp.exp2(scores - jnp.max(scores, axis=1, keepdims=True))
        total = jnp.sum(weights, axis=1, keepdims=True)
        mixed = jnp.dot(
            weights.astype(jnp.bfloat16), v_buf[head, keys, :], preferred_element_type=jnp.float32
        )
        o_buf[head, rows, :] = (mixed / total).astype(jnp.bfloat16)
        columns = pl.ds(pl.multiple_of(me * HEADS * HEAD_DIM + head * HEAD_DIM, LANES), HEAD_DIM)
        source, target = o_buf.at[head, rows, :], out_ref.at[:, columns]

        @pl.when(strip == me)
        def _():
            pltpu.make_async_copy(source, target, out_recv).start()

        @pl.when(strip != me)
        def _():
            pltpu.make_async_remote_copy(
                src_ref=source,
                dst_ref=target,
                send_sem=out_send,
                recv_sem=out_recv,
                device_id=member(strip),
                device_id_type=MESH,
            ).start()

    for group in range(DEPTH):
        start_group(group)

    edge = jnp.zeros((HEADS, 64, HEAD_DIM), jnp.bfloat16)
    for buffer in (k_buf, v_buf):
        buffer[:, 0 : FRONT - BACK, :] = edge
        buffer[:, FRONT + BLOCK + AHEAD : WINDOW, :] = edge

    @pl.when(block == 0)
    def _():
        for buffer in (k_buf, v_buf):
            buffer[:, FRONT - BACK : FRONT, :] = jnp.zeros((HEADS, BACK, HEAD_DIM), jnp.bfloat16)

    @pl.when(block == BLOCKS - 1)
    def _():
        for buffer in (k_buf, v_buf):
            buffer[:, FRONT + BLOCK : FRONT + BLOCK + AHEAD, :] = jnp.zeros((HEADS, AHEAD, HEAD_DIM), jnp.bfloat16)

    for group in range(2 * HEADS):
        wait_group(group)
        start_halo(*divmod(group, HEADS))
        start_group(group + DEPTH)
        totals_step(group)
        make_bias(group)

    for head in range(HEADS):
        for array in range(2):
            wait_halo(array, head)
        group = 2 * HEADS + head
        wait_group(group)
        if group + DEPTH < 3 * HEADS:
            start_group(group + DEPTH)

        def step(i, carry, head=head):
            attend(head, lax.rem(me + i, GROUP))
            return carry

        lax.fori_loop(1, GROUP + 1, step, 0)
        if head < 2:
            totals_step(2 * HEADS + head)

    for array in range(3):
        drain(targets[array].at[:, pl.ds(0, BLOCK - STRIP), :], in_send.at[array])
    for array in range(2):
        drain_halo(array)
    for number, slots, size in ((0, slots_a, GROUP), (1, slots_b, NY)):
        drain(slots.at[pl.ds(0, size - 1)], stat_send.at[number])
    for number in range(NZ - 1):
        relay_drain(number)
    drain(o_buf.at[:, pl.ds(0, BLOCK - STRIP), :], out_send)
    drain(out_ref, out_recv)


def store_kernel(chunks, attended, counts, losses, attended_out, counts_out, losses_out, sems):
    rows = attended.shape[0] // chunks
    parts = [(attended.at[pl.ds(i * rows, rows)], attended_out.at[pl.ds(i * rows, rows)]) for i in range(chunks)]
    parts += [(counts, counts_out), (losses, losses_out)]
    copies = [pltpu.make_async_copy(source, target, sems.at[i]) for i, (source, target) in enumerate(parts)]
    for copy in copies:
        copy.start()
    for copy in copies:
        copy.wait()


def store(attended, counts, losses, chunks=4):
    local = pl.BlockSpec(memory_space=pltpu.VMEM)
    anywhere = pl.BlockSpec(memory_space=pl.ANY)
    results = (attended, counts, losses)
    return pl.pallas_call(
        functools.partial(store_kernel, chunks),
        name="store_results",
        out_shape=tuple(jax.ShapeDtypeStruct(a.shape, a.dtype) for a in results),
        in_specs=[local] * 3,
        out_specs=(anywhere,) * 3,
        scratch_shapes=[pltpu.SemaphoreType.DMA((chunks + 2,))],
    )(*(pltpu.with_memory_space_constraint(a, pltpu.VMEM) for a in results))


def per_device(queries, key_rows, values, doc_ids, image_flags, labels, token_loss):
    documents = doc_ids.shape[0] // DOC_MEAN
    id_shape = (BLOCKS * BLOCK // LANES, LANES)
    anywhere = pl.BlockSpec(memory_space=pl.ANY)
    local = pl.BlockSpec(memory_space=pltpu.VMEM)
    window = pltpu.VMEM((HEADS, WINDOW, HEAD_DIM), jnp.bfloat16)
    own = pltpu.VMEM((HEADS, BLOCK, HEAD_DIM), jnp.bfloat16)
    attended, counts, losses = pl.pallas_call(
        kernel,
        name="exchange_and_attend",
        out_shape=(
            pltpu.VMEM(queries.shape, jnp.bfloat16),
            pltpu.VMEM((1, LANES), jnp.float32),
            pltpu.VMEM((1, LANES), jnp.float32),
        ),
        in_specs=[anywhere] * 7,
        out_specs=(local, local, local),
        scratch_shapes=[
            own,
            window,
            window,
            own,
            pltpu.VMEM((BLOCK, SPAN), jnp.float32),
            pltpu.VMEM(id_shape, jnp.int32),
            pltpu.VMEM(id_shape, jnp.int32),
            pltpu.VMEM((BLOCK, LANES), jnp.int32),
            pltpu.VMEM((BLOCK, LANES), jnp.int32),
            pltpu.VMEM((GROUP, 8, LANES), jnp.float32),
            pltpu.VMEM((NY, 8, LANES), jnp.float32),
            pltpu.VMEM((NZ, 8, LANES), jnp.float32),
            pltpu.VMEM((1, STRIP), jnp.int32),
            pltpu.VMEM((1, STRIP), jnp.float32),
            pltpu.SemaphoreType.DMA((4,)),
            pltpu.SemaphoreType.DMA((3,)),
            pltpu.SemaphoreType.DMA((3, HEADS)),
            pltpu.SemaphoreType.DMA((2,)),
            pltpu.SemaphoreType.DMA((2, HEADS)),
            pltpu.SemaphoreType.DMA((2,)),
            pltpu.SemaphoreType.DMA((2, HEADS)),
            pltpu.SemaphoreType.DMA,
            pltpu.SemaphoreType.DMA,
            pltpu.SemaphoreType.DMA((2,)),
            pltpu.SemaphoreType.DMA((2,)),
            pltpu.SemaphoreType.DMA((2, NZ - 1)),
            pltpu.SemaphoreType.DMA((2, NZ - 1)),
        ],
        compiler_params=pltpu.CompilerParams(
            collective_id=0, has_side_effects=True, vmem_limit_bytes=40 * 1024 * 1024
        ),
    )(
        *(
            pltpu.with_memory_space_constraint(array, pltpu.HBM)
            for array in (
                queries,
                key_rows,
                values,
                doc_ids.reshape(id_shape),
                image_flags.reshape(id_shape),
                labels.reshape(1, STRIP),
                token_loss.reshape(1, STRIP),
            )
        )
    )
    attended, counts, losses = store(attended, counts, losses)
    return attended, counts.reshape(documents), losses.reshape(documents)


def solution(mesh):
    split = Mesh(mesh.devices.reshape(NZ, NY, NC, NX), AXES)
    return jax.shard_map(
        per_device,
        mesh=split,
        in_specs=(
            P(AXES, None),
            P(AXES, None),
            P(AXES, None),
            P(),
            P(),
            P(AXES),
            P(AXES),
        ),
        out_specs=(P(AXES, None), P(), P()),
        check_vma=False,
    )
```

```python
import functools
import math

import jax
import jax.numpy as jnp
from jax import lax
from jax.experimental import pallas as pl
from jax.experimental.pallas import tpu as pltpu
from jax.sharding import Mesh
from jax.sharding import PartitionSpec as P

HEAD_DIM = 128
DOC_MEAN = 384
NZ, NY, NC, NX = 8, 4, 2, 4
GROUP = NC * NX
STRIP = 192
BLOCK = STRIP * GROUP
BLOCKS = NZ * NY
HEADS = 4
BACK, AHEAD = 704, 576
FRONT = 768
SPAN = 1536
WINDOW = FRONT + BLOCK + 640
DEPTH = 3
LANES = 128
AXES = ("z", "y", "c", "x")
MESH = pl.DeviceIdType.MESH


def first_key(strip):
    return pl.multiple_of(((3 * strip + 1) // 2) * LANES, LANES)


def kernel(
    q_hbm,
    k_hbm,
    v_hbm,
    docs_hbm,
    flags_hbm,
    labels_hbm,
    token_loss_hbm,
    out_ref,
    count_ref,
    loss_ref,
    q_buf,
    k_buf,
    v_buf,
    o_buf,
    bias,
    docs,
    flags,
    q_docs,
    q_images,
    slots_a,
    slots_b,
    slots_c,
    labels,
    token_loss,
    id_sem,
    in_send,
    in_recv,
    back_send,
    back_recv,
    ahead_send,
    ahead_recv,
    out_send,
    out_recv,
    stat_send,
    stat_recv,
    relay_send,
    relay_recv,
    met_far,
    met_upper,
):
    z, y, c, x = (lax.axis_index(name) for name in AXES)
    me = c * NX + x
    block = z * NY + y
    has_after, has_before = block < BLOCKS - 1, block > 0
    after = lax.rem(block + 1, BLOCKS)
    before = lax.rem(block + BLOCKS - 1, BLOCKS)
    has_upper, has_lower = z < NZ - 1, z > 0
    upper, lower = lax.rem(z + 1, NZ), lax.rem(z + NZ - 1, NZ)

    def member(index):
        return {"z": z, "y": y, "c": lax.div(index, NX), "x": lax.rem(index, NX)}

    def in_block(index):
        return {"z": lax.div(index, NY), "y": lax.rem(index, NY), "c": c, "x": x}

    def along_y(index):
        return {"z": z, "y": index, "c": c, "x": x}

    def along_z(index):
        return {"z": index, "y": y, "c": c, "x": x}

    id_copies = [
        pltpu.make_async_copy(docs_hbm, docs, id_sem.at[0]),
        pltpu.make_async_copy(flags_hbm, flags, id_sem.at[1]),
        pltpu.make_async_copy(labels_hbm, labels, id_sem.at[2]),
        pltpu.make_async_copy(token_loss_hbm, token_loss, id_sem.at[3]),
    ]
    for copy in id_copies:
        copy.start()

    barrier = pltpu.get_barrier_semaphore()
    def toward(steps, other):
        return lax.rem(c + other, NC) * NX + lax.rem(x + steps, NX)

    def tell(sem, present, peer):
        def signal():
            pl.semaphore_signal(sem, inc=1, device_id=peer, device_id_type=MESH)

        if present is None:
            signal()
        else:
            pl.when(present)(signal)

    for steps, other in ((1, 0), (NX - 1, 0), (1, 1), (NX - 1, 1), (0, 1)):
        tell(barrier, None, member(toward(steps, other)))
    for o in range(NY):
        tell(barrier, y < o, along_y(o))
    tell(barrier, has_upper, along_z(upper))
    tell(barrier, has_upper & (y == NY - 1), in_block(after))
    from_lower = jnp.where(has_lower, jnp.where(y == 0, 2, 1), 0) + y
    from_upper = jnp.where(has_upper, jnp.where(y == NY - 1, 2, 1), 0) + NY - 1 - y
    pl.semaphore_wait(barrier, 5 + from_lower)
    tell(met_far, None, member(toward(1, 0)))
    for o in range(NY):
        tell(met_upper, y > o, along_y(o))
    tell(met_upper, has_lower, along_z(lower))
    tell(met_upper, has_lower & (y == 0), in_block(before))

    def drain(ref, sem):
        pltpu.make_async_copy(ref, ref, sem).wait()

    sources = (k_hbm, v_hbm, q_hbm)
    targets = (k_buf, v_buf, q_buf)
    bases = (FRONT, FRONT, 0)

    def piece(array, head, owner):
        columns = pl.ds(pl.multiple_of(owner * HEADS * HEAD_DIM + head * HEAD_DIM, LANES), HEAD_DIM)
        rows = pl.ds(pl.multiple_of(bases[array] + me * STRIP, 64), STRIP)
        return sources[array].at[:, columns], targets[array].at[head, rows, :]

    def start_group(group):
        array, head = divmod(group, HEADS)

        def send(owner):
            source, target = piece(array, head, owner)
            pltpu.make_async_remote_copy(
                src_ref=source,
                dst_ref=target,
                send_sem=in_send.at[array],
                recv_sem=in_recv.at[array, head],
                device_id=member(owner),
                device_id_type=MESH,
            ).start()

        def near(o, carry):
            send(toward(1 + (NX - 2) * lax.rem(o, 2), lax.div(o, 2)))
            return carry

        def far(o, carry):
            send(toward(2, o))
            return carry

        lax.fori_loop(0, 2 * NC, near, 0)
        if group == 0:
            pl.semaphore_wait(met_far, 1)
        lax.fori_loop(0, NC, far, 0)
        send(toward(0, 1))
        source, target = piece(array, head, me)
        pltpu.make_async_copy(source, target, in_recv.at[array, head]).start()

    def wait_group(group):
        array, head = divmod(group, HEADS)
        rows = targets[array].at[head, pl.ds(bases[array], BLOCK), :]
        pltpu.make_async_copy(rows, rows, in_recv.at[array, head]).wait()

    def halos(array, head):
        return (
            (has_after, has_before, BACK, FRONT + BLOCK - BACK, FRONT - BACK, after, back_send, back_recv),
            (has_before, has_after, AHEAD, FRONT, FRONT + BLOCK, before, ahead_send, ahead_recv),
        )

    def start_halo(array, head):
        buffer = targets[array]
        for sends, _, rows, first, target, peer, send_sem, recv_sem in halos(array, head):

            @pl.when(sends)
            def _():
                pltpu.make_async_remote_copy(
                    src_ref=buffer.at[head, pl.ds(first, rows), :],
                    dst_ref=buffer.at[head, pl.ds(target, rows), :],
                    send_sem=send_sem.at[array],
                    recv_sem=recv_sem.at[array, head],
                    device_id=in_block(peer),
                    device_id_type=MESH,
                ).start()

    def wait_halo(array, head):
        for _, receives, rows, _, target, _, _, recv_sem in halos(array, head):

            @pl.when(receives)
            def _():
                drain(targets[array].at[head, pl.ds(target, rows), :], recv_sem.at[array, head])

    def drain_halo(array):
        for sends, _, rows, _, _, _, send_sem, _ in halos(array, 0):

            @pl.when(sends)
            def _():
                drain(targets[array].at[:, pl.ds(0, rows), :], send_sem.at[array])

    def stage_send(number, slots, own, size, peer_of):
        def send(o, carry):
            pltpu.make_async_remote_copy(
                src_ref=slots.at[own],
                dst_ref=slots.at[own],
                send_sem=stat_send.at[number],
                recv_sem=stat_recv.at[number],
                device_id=peer_of(lax.rem(own + o, size)),
                device_id_type=MESH,
            ).start()
            return carry

        lax.fori_loop(1, size, send, 0)

    def stage_sum(number, slots, size):
        others = slots.at[pl.ds(0, size - 1)]
        pltpu.make_async_copy(others, others, stat_recv.at[number]).wait()
        total = slots[0]
        for i in range(1, size):
            total = total + slots[i]
        return total

    def relays(step):
        return (
            (has_upper & (z >= step), z - step, has_lower & (z >= step + 1), z - 1 - step, upper, 0),
            (has_lower & (z + step < NZ), z + step, has_upper & (z + step + 1 < NZ), z + 1 + step, lower, 1),
        )

    def relay_copy(step, slot, peer, way):
        return pltpu.make_async_remote_copy(
            src_ref=slots_c.at[slot],
            dst_ref=slots_c.at[slot],
            send_sem=relay_send.at[way, step],
            recv_sem=relay_recv.at[way, step],
            device_id=along_z(peer),
            device_id_type=MESH,
        )

    def relay_start(step):
        for sends, slot, _, _, peer, way in relays(step):

            @pl.when(sends)
            def _():
                relay_copy(step, slot, peer, way).start()

    def relay_wait(step):
        for _, _, receives, slot, peer, way in relays(step):

            @pl.when(receives)
            def _():
                drain(slots_c.at[slot], relay_recv.at[way, step])

    def relay_drain(step):
        for sends, slot, _, _, peer, way in relays(step):

            @pl.when(sends)
            def _():
                drain(slots_c.at[slot], relay_send.at[way, step])

    def document_partials():
        first = lax.div(block * BLOCK + me * STRIP, LANES)
        pair = jnp.concatenate([docs[pl.ds(first, 1), :], docs[pl.ds(first + 1, 1), :]], axis=1)
        half = jnp.concatenate([pair[:, 64:], pair[:, :64]], axis=1)
        doc = jnp.where(lax.rem(me, 2) == 1, half, pair)[:, :STRIP]
        weight = jnp.where(labels[...] >= 0, 1.0, 0.0)
        lines = lax.broadcasted_iota(jnp.int32, (8, STRIP), 0)
        terms = jnp.where(lines == 0, weight, jnp.where(lines == 1, weight * token_loss[...], 0.0))
        hit = jnp.where(lax.broadcasted_iota(jnp.int32, (LANES, STRIP), 0) == doc, 1.0, 0.0)
        return lax.dot_general(
            terms,
            hit,
            (((1,), (1,)), ((), ())),
            precision=lax.Precision.HIGHEST,
            preferred_element_type=jnp.float32,
        )

    def totals_step(point):
        if point == 0:
            for copy in id_copies:
                copy.wait()
            slots_a[me] = document_partials()
            stage_send(0, slots_a, me, GROUP, member)
            make_query_ids()
        elif point == 1:
            slots_b[y] = stage_sum(0, slots_a, GROUP)
            stage_send(1, slots_b, y, NY, along_y)
        elif point == 2:
            slots_c[z] = stage_sum(1, slots_b, NY)
            relay_start(0)
        else:
            relay_wait(point - 3)
            if point - 2 < NZ - 1:
                relay_start(point - 2)
            else:
                total = slots_c[0]
                for i in range(1, NZ):
                    total = total + slots_c[i]
                counts = total[0:1]
                count_ref[...] = counts
                loss_ref[...] = total[1:2] / jnp.maximum(counts, 1.0)

    def id_row(row):
        at = pl.ds(lax.rem(block * (BLOCK // LANES) + row + BLOCKS * (BLOCK // LANES), BLOCKS * (BLOCK // LANES)), 1)
        doc = docs[at, :]
        return doc, jnp.where(flags[at, :] == 1, doc, -1)

    def make_query_ids():
        def one(row, carry):
            at = pl.ds(pl.multiple_of(row * LANES, LANES), LANES)
            doc, image = id_row(row)
            q_docs[at, :] = jnp.broadcast_to(doc, (LANES, LANES)).T
            q_images[at, :] = jnp.broadcast_to(image, (LANES, LANES)).T
            return carry

        lax.fori_loop(0, BLOCK // LANES, one, 0)

    def make_bias(strip):
        start = first_key(strip)
        rows = pl.ds(pl.multiple_of(strip * STRIP, 64), STRIP)
        doc, image = q_docs[rows, :], q_images[rows, :]
        shape = (STRIP, LANES)
        offset = lax.broadcasted_iota(jnp.int32, shape, 1) - lax.broadcasted_iota(jnp.int32, shape, 0)
        first_row = lax.div(start, LANES) - FRONT // LANES
        for i in range(SPAN // LANES):
            key_doc, key_image = id_row(first_row + i)
            key_image = jnp.where(key_image < 0, -2, key_image)
            earlier = offset <= FRONT + strip * STRIP - start - i * LANES
            allowed = ((doc == key_doc) & earlier) | (image == key_image)
            bias[rows, i * LANES : (i + 1) * LANES] = jnp.where(allowed, 0.0, -jnp.inf)

    def attend(head, strip):
        start = first_key(strip)
        rows = pl.ds(pl.multiple_of(strip * STRIP, 64), STRIP)
        keys = pl.ds(start, SPAN)
        scores = lax.dot_general(
            q_buf[head, rows, :],
            k_buf[head, keys, :],
            (((1,), (1,)), ((), ())),
            preferred_element_type=jnp.float32,
        )
        scores = scores * (HEAD_DIM**-0.5 * math.log2(math.e)) + bias[rows, :]
        weights = jnp.exp2(scores - jnp.max(scores, axis=1, keepdims=True))
        total = jnp.sum(weights, axis=1, keepdims=True)
        mixed = jnp.dot(
            weights.astype(jnp.bfloat16), v_buf[head, keys, :], preferred_element_type=jnp.float32
        )
        o_buf[head, rows, :] = (mixed / total).astype(jnp.bfloat16)
        columns = pl.ds(pl.multiple_of(me * HEADS * HEAD_DIM + head * HEAD_DIM, LANES), HEAD_DIM)
        source, target = o_buf.at[head, rows, :], out_ref.at[:, columns]

        @pl.when(strip == me)
        def _():
            pltpu.make_async_copy(source, target, out_recv).start()

        @pl.when(strip != me)
        def _():
            pltpu.make_async_remote_copy(
                src_ref=source,
                dst_ref=target,
                send_sem=out_send,
                recv_sem=out_recv,
                device_id=member(strip),
                device_id_type=MESH,
            ).start()

    for group in range(DEPTH):
        start_group(group)

    edge = jnp.zeros((HEADS, 64, HEAD_DIM), jnp.bfloat16)
    for buffer in (k_buf, v_buf):
        buffer[:, 0 : FRONT - BACK, :] = edge
        buffer[:, FRONT + BLOCK + AHEAD : WINDOW, :] = edge

    @pl.when(block == 0)
    def _():
        for buffer in (k_buf, v_buf):
            buffer[:, FRONT - BACK : FRONT, :] = jnp.zeros((HEADS, BACK, HEAD_DIM), jnp.bfloat16)

    @pl.when(block == BLOCKS - 1)
    def _():
        for buffer in (k_buf, v_buf):
            buffer[:, FRONT + BLOCK : FRONT + BLOCK + AHEAD, :] = jnp.zeros((HEADS, AHEAD, HEAD_DIM), jnp.bfloat16)

    for group in range(2 * HEADS):
        wait_group(group)
        if group == 0:

            @pl.when(from_upper > 0)
            def _():
                pl.semaphore_wait(met_upper, from_upper)

        start_halo(*divmod(group, HEADS))
        start_group(group + DEPTH)
        totals_step(group)
        make_bias(group)

    for head in range(HEADS):
        for array in range(2):
            wait_halo(array, head)
        group = 2 * HEADS + head
        wait_group(group)
        if group + DEPTH < 3 * HEADS:
            start_group(group + DEPTH)

        def step(i, carry, head=head):
            attend(head, lax.rem(me + i, GROUP))
            return carry

        lax.fori_loop(1, GROUP + 1, step, 0)
        if head < 2:
            totals_step(2 * HEADS + head)

    for array in range(3):
        drain(targets[array].at[:, pl.ds(0, BLOCK - STRIP), :], in_send.at[array])
    for array in range(2):
        drain_halo(array)
    for number, slots, size in ((0, slots_a, GROUP), (1, slots_b, NY)):
        drain(slots.at[pl.ds(0, size - 1)], stat_send.at[number])
    for number in range(NZ - 1):
        relay_drain(number)
    drain(o_buf.at[:, pl.ds(0, BLOCK - STRIP), :], out_send)
    drain(out_ref, out_recv)


def store_kernel(chunks, attended, counts, losses, attended_out, counts_out, losses_out, sems):
    rows = attended.shape[0] // chunks
    parts = [(attended.at[pl.ds(i * rows, rows)], attended_out.at[pl.ds(i * rows, rows)]) for i in range(chunks)]
    parts += [(counts, counts_out), (losses, losses_out)]
    copies = [pltpu.make_async_copy(source, target, sems.at[i]) for i, (source, target) in enumerate(parts)]
    for copy in copies:
        copy.start()
    for copy in copies:
        copy.wait()


def store(attended, counts, losses, chunks=4):
    local = pl.BlockSpec(memory_space=pltpu.VMEM)
    anywhere = pl.BlockSpec(memory_space=pl.ANY)
    results = (attended, counts, losses)
    return pl.pallas_call(
        functools.partial(store_kernel, chunks),
        name="store_results",
        out_shape=tuple(jax.ShapeDtypeStruct(a.shape, a.dtype) for a in results),
        in_specs=[local] * 3,
        out_specs=(anywhere,) * 3,
        scratch_shapes=[pltpu.SemaphoreType.DMA((chunks + 2,))],
    )(*(pltpu.with_memory_space_constraint(a, pltpu.VMEM) for a in results))


def per_device(queries, key_rows, values, doc_ids, image_flags, labels, token_loss):
    documents = doc_ids.shape[0] // DOC_MEAN
    id_shape = (BLOCKS * BLOCK // LANES, LANES)
    anywhere = pl.BlockSpec(memory_space=pl.ANY)
    local = pl.BlockSpec(memory_space=pltpu.VMEM)
    window = pltpu.VMEM((HEADS, WINDOW, HEAD_DIM), jnp.bfloat16)
    own = pltpu.VMEM((HEADS, BLOCK, HEAD_DIM), jnp.bfloat16)
    attended, counts, losses = pl.pallas_call(
        kernel,
        name="exchange_and_attend",
        out_shape=(
            pltpu.VMEM(queries.shape, jnp.bfloat16),
            pltpu.VMEM((1, LANES), jnp.float32),
            pltpu.VMEM((1, LANES), jnp.float32),
        ),
        in_specs=[anywhere] * 7,
        out_specs=(local, local, local),
        scratch_shapes=[
            own,
            window,
            window,
            own,
            pltpu.VMEM((BLOCK, SPAN), jnp.float32),
            pltpu.VMEM(id_shape, jnp.int32),
            pltpu.VMEM(id_shape, jnp.int32),
            pltpu.VMEM((BLOCK, LANES), jnp.int32),
            pltpu.VMEM((BLOCK, LANES), jnp.int32),
            pltpu.VMEM((GROUP, 8, LANES), jnp.float32),
            pltpu.VMEM((NY, 8, LANES), jnp.float32),
            pltpu.VMEM((NZ, 8, LANES), jnp.float32),
            pltpu.VMEM((1, STRIP), jnp.int32),
            pltpu.VMEM((1, STRIP), jnp.float32),
            pltpu.SemaphoreType.DMA((4,)),
            pltpu.SemaphoreType.DMA((3,)),
            pltpu.SemaphoreType.DMA((3, HEADS)),
            pltpu.SemaphoreType.DMA((2,)),
            pltpu.SemaphoreType.DMA((2, HEADS)),
            pltpu.SemaphoreType.DMA((2,)),
            pltpu.SemaphoreType.DMA((2, HEADS)),
            pltpu.SemaphoreType.DMA,
            pltpu.SemaphoreType.DMA,
            pltpu.SemaphoreType.DMA((2,)),
            pltpu.SemaphoreType.DMA((2,)),
            pltpu.SemaphoreType.DMA((2, NZ - 1)),
            pltpu.SemaphoreType.DMA((2, NZ - 1)),
            pltpu.SemaphoreType.REGULAR,
            pltpu.SemaphoreType.REGULAR,
        ],
        compiler_params=pltpu.CompilerParams(
            collective_id=0, has_side_effects=True, vmem_limit_bytes=40 * 1024 * 1024
        ),
    )(
        *(
            pltpu.with_memory_space_constraint(array, pltpu.HBM)
            for array in (
                queries,
                key_rows,
                values,
                doc_ids.reshape(id_shape),
                image_flags.reshape(id_shape),
                labels.reshape(1, STRIP),
                token_loss.reshape(1, STRIP),
            )
        )
    )
    attended, counts, losses = store(attended, counts, losses)
    return attended, counts.reshape(documents), losses.reshape(documents)


def solution(mesh):
    split = Mesh(mesh.devices.reshape(NZ, NY, NC, NX), AXES)
    return jax.shard_map(
        per_device,
        mesh=split,
        in_specs=(
            P(AXES, None),
            P(AXES, None),
            P(AXES, None),
            P(),
            P(),
            P(AXES),
            P(AXES),
        ),
        out_specs=(P(AXES, None), P(), P()),
        check_vma=False,
    )
```

```python
import functools
import math

import jax
import jax.numpy as jnp
from jax import lax
from jax.experimental import pallas as pl
from jax.experimental.pallas import tpu as pltpu
from jax.sharding import Mesh
from jax.sharding import PartitionSpec as P

HEAD_DIM = 128
DOC_MEAN = 384
NZ, NY, NC, NX = 8, 4, 2, 4
GROUP = NC * NX
STRIP = 192
BLOCK = STRIP * GROUP
BLOCKS = NZ * NY
HEADS = 4
BACK, AHEAD = 704, 576
FRONT = 768
SPAN = 1536
WINDOW = FRONT + BLOCK + 640
LANES = 128
AXES = ("z", "y", "c", "x")
MESH = pl.DeviceIdType.MESH


def first_key(strip):
    return pl.multiple_of(((3 * strip + 1) // 2) * LANES, LANES)


def kernel(
    q_hbm,
    k_hbm,
    v_hbm,
    docs_hbm,
    flags_hbm,
    labels_hbm,
    token_loss_hbm,
    out_ref,
    count_ref,
    loss_ref,
    q_buf,
    k_buf,
    v_buf,
    o_buf,
    bias,
    docs,
    flags,
    q_docs,
    q_images,
    slots_a,
    slots_b,
    slots_c,
    labels,
    token_loss,
    stage,
    stage_sem,
    id_sem,
    in_send,
    in_recv,
    back_send,
    back_recv,
    ahead_send,
    ahead_recv,
    out_send,
    out_recv,
    stat_send,
    stat_recv,
    relay_send,
    relay_recv,
    met_far,
    met_upper,
):
    z, y, c, x = (lax.axis_index(name) for name in AXES)
    me = c * NX + x
    block = z * NY + y
    has_after, has_before = block < BLOCKS - 1, block > 0
    after = lax.rem(block + 1, BLOCKS)
    before = lax.rem(block + BLOCKS - 1, BLOCKS)
    has_upper, has_lower = z < NZ - 1, z > 0
    upper, lower = lax.rem(z + 1, NZ), lax.rem(z + NZ - 1, NZ)

    def member(index):
        return {"z": z, "y": y, "c": lax.div(index, NX), "x": lax.rem(index, NX)}

    def in_block(index):
        return {"z": lax.div(index, NY), "y": lax.rem(index, NY), "c": c, "x": x}

    def along_y(index):
        return {"z": z, "y": index, "c": c, "x": x}

    def along_z(index):
        return {"z": index, "y": y, "c": c, "x": x}

    id_copies = [
        pltpu.make_async_copy(docs_hbm, docs, id_sem.at[0]),
        pltpu.make_async_copy(flags_hbm, flags, id_sem.at[1]),
        pltpu.make_async_copy(labels_hbm, labels, id_sem.at[2]),
        pltpu.make_async_copy(token_loss_hbm, token_loss, id_sem.at[3]),
    ]
    stage_copies = [
        pltpu.make_async_copy(source, stage.at[array], stage_sem.at[array])
        for array, source in enumerate((k_hbm, v_hbm, q_hbm))
    ]
    for copy in stage_copies:
        copy.start()

    barrier = pltpu.get_barrier_semaphore()
    def toward(steps, other):
        return lax.rem(c + other, NC) * NX + lax.rem(x + steps, NX)

    def tell(sem, present, peer):
        def signal():
            pl.semaphore_signal(sem, inc=1, device_id=peer, device_id_type=MESH)

        if present is None:
            signal()
        else:
            pl.when(present)(signal)

    def meet_near(o, carry):
        tell(barrier, None, member(toward(jnp.where(o == 4, 0, 1 + (NX - 2) * lax.rem(o, 2)), jnp.where(o < 2, 0, 1))))
        return carry

    def meet_higher(o, carry):
        tell(barrier, None, along_y(o))
        return carry

    def answer_lower(o, carry):
        tell(met_upper, None, along_y(o))
        return carry

    lax.fori_loop(0, 5, meet_near, 0)
    lax.fori_loop(y + 1, NY, meet_higher, 0)
    tell(barrier, has_upper, along_z(upper))
    tell(barrier, has_upper & (y == NY - 1), in_block(after))
    from_lower = jnp.where(has_lower, jnp.where(y == 0, 2, 1), 0) + y
    from_upper = jnp.where(has_upper, jnp.where(y == NY - 1, 2, 1), 0) + NY - 1 - y
    pl.semaphore_wait(barrier, 5 + from_lower)
    tell(met_far, None, member(toward(1, 0)))

    def drain(ref, sem):
        pltpu.make_async_copy(ref, ref, sem).wait()

    targets = (k_buf, v_buf, q_buf)
    bases = (FRONT, FRONT, 0)

    def piece(array, head, owner):
        columns = pl.ds(pl.multiple_of(owner * HEADS * HEAD_DIM + head * HEAD_DIM, LANES), HEAD_DIM)
        rows = pl.ds(pl.multiple_of(bases[array] + me * STRIP, 64), STRIP)
        return stage.at[array, :, columns], targets[array].at[head, rows, :]

    def start_group(array, head, first=None):
        def send(owner):
            source, target = piece(array, head, owner)
            pltpu.make_async_remote_copy(
                src_ref=source,
                dst_ref=target,
                send_sem=in_send.at[array],
                recv_sem=in_recv.at[array, head],
                device_id=member(owner),
                device_id_type=MESH,
            ).start()

        def near(o, carry):
            send(toward(1 + (NX - 2) * lax.rem(o, 2), lax.div(o, 2)))
            return carry

        def far(o, carry):
            send(toward(2, o))
            return carry

        lax.fori_loop(0, 2 * NC, near, 0)
        if first is not None:

            @pl.when(first)
            def _():
                pl.semaphore_wait(met_far, 1)

        lax.fori_loop(0, NC, far, 0)
        send(toward(0, 1))
        source, target = piece(array, head, me)
        pltpu.make_async_copy(source, target, in_recv.at[array, head]).start()

    def wait_group(array, head):
        rows = targets[array].at[head, pl.ds(bases[array], BLOCK), :]
        pltpu.make_async_copy(rows, rows, in_recv.at[array, head]).wait()

    def halos(array, head):
        return (
            (has_after, has_before, BACK, FRONT + BLOCK - BACK, FRONT - BACK, after, back_send, back_recv),
            (has_before, has_after, AHEAD, FRONT, FRONT + BLOCK, before, ahead_send, ahead_recv),
        )

    def start_halo(array, head):
        buffer = targets[array]
        for sends, _, rows, first, target, peer, send_sem, recv_sem in halos(array, head):

            @pl.when(sends)
            def _():
                pltpu.make_async_remote_copy(
                    src_ref=buffer.at[head, pl.ds(first, rows), :],
                    dst_ref=buffer.at[head, pl.ds(target, rows), :],
                    send_sem=send_sem.at[array],
                    recv_sem=recv_sem.at[array, head],
                    device_id=in_block(peer),
                    device_id_type=MESH,
                ).start()

    def wait_halo(array, head):
        for _, receives, rows, _, target, _, _, recv_sem in halos(array, head):

            @pl.when(receives)
            def _():
                drain(targets[array].at[head, pl.ds(target, rows), :], recv_sem.at[array, head])

    def drain_halo(array):
        for sends, _, rows, _, _, _, send_sem, _ in halos(array, 0):

            @pl.when(sends)
            def _():
                drain(targets[array].at[:, pl.ds(0, rows), :], send_sem.at[array])

    def stage_send(number, slots, own, size, peer_of):
        def send(o, carry):
            pltpu.make_async_remote_copy(
                src_ref=slots.at[own],
                dst_ref=slots.at[own],
                send_sem=stat_send.at[number],
                recv_sem=stat_recv.at[number],
                device_id=peer_of(lax.rem(own + o, size)),
                device_id_type=MESH,
            ).start()
            return carry

        lax.fori_loop(1, size, send, 0)

    def stage_sum(number, slots, size):
        others = slots.at[pl.ds(0, size - 1)]
        pltpu.make_async_copy(others, others, stat_recv.at[number]).wait()
        total = slots[0]
        for i in range(1, size):
            total = total + slots[i]
        return total

    def relays(step):
        return (
            (has_upper & (z >= step), z - step, has_lower & (z >= step + 1), z - 1 - step, upper, 0),
            (has_lower & (z + step < NZ), z + step, has_upper & (z + step + 1 < NZ), z + 1 + step, lower, 1),
        )

    def relay_copy(step, slot, peer, way):
        return pltpu.make_async_remote_copy(
            src_ref=slots_c.at[slot],
            dst_ref=slots_c.at[slot],
            send_sem=relay_send.at[way, step],
            recv_sem=relay_recv.at[way, step],
            device_id=along_z(peer),
            device_id_type=MESH,
        )

    def relay_start(step):
        for sends, slot, _, _, peer, way in relays(step):

            @pl.when(sends)
            def _():
                relay_copy(step, slot, peer, way).start()

    def relay_wait(step):
        for _, _, receives, slot, peer, way in relays(step):

            @pl.when(receives)
            def _():
                drain(slots_c.at[slot], relay_recv.at[way, step])

    def relay_drain(step):
        for sends, slot, _, _, peer, way in relays(step):

            @pl.when(sends)
            def _():
                drain(slots_c.at[slot], relay_send.at[way, step])

    def document_partials():
        first = lax.div(block * BLOCK + me * STRIP, LANES)
        pair = jnp.concatenate([docs[pl.ds(first, 1), :], docs[pl.ds(first + 1, 1), :]], axis=1)
        half = jnp.concatenate([pair[:, 64:], pair[:, :64]], axis=1)
        doc = jnp.where(lax.rem(me, 2) == 1, half, pair)[:, :STRIP]
        weight = jnp.where(labels[...] >= 0, 1.0, 0.0)
        lines = lax.broadcasted_iota(jnp.int32, (8, STRIP), 0)
        terms = jnp.where(lines == 0, weight, jnp.where(lines == 1, weight * token_loss[...], 0.0))
        hit = jnp.where(lax.broadcasted_iota(jnp.int32, (LANES, STRIP), 0) == doc, 1.0, 0.0)
        return lax.dot_general(
            terms,
            hit,
            (((1,), (1,)), ((), ())),
            precision=lax.Precision.HIGHEST,
            preferred_element_type=jnp.float32,
        )

    def totals_start(head):
        @pl.when(head == 0)
        def _():
            for copy in id_copies:
                copy.wait()
            slots_a[me] = document_partials()
            stage_send(0, slots_a, me, GROUP, member)
            make_query_ids()

        @pl.when(head == 1)
        def _():
            slots_b[y] = stage_sum(0, slots_a, GROUP)
            stage_send(1, slots_b, y, NY, along_y)

        @pl.when(head == 2)
        def _():
            slots_c[z] = stage_sum(1, slots_b, NY)
            relay_start(0)

        @pl.when(head == 3)
        def _():
            relay_wait(0)
            relay_start(1)

    def totals_end():
        total = slots_c[0]
        for i in range(1, NZ):
            total = total + slots_c[i]
        counts = total[0:1]
        count_ref[...] = counts
        loss_ref[...] = total[1:2] / jnp.maximum(counts, 1.0)

    def id_row(row):
        at = pl.ds(lax.rem(block * (BLOCK // LANES) + row + BLOCKS * (BLOCK // LANES), BLOCKS * (BLOCK // LANES)), 1)
        doc = docs[at, :]
        return doc, jnp.where(flags[at, :] == 1, doc, -1)

    def make_query_ids():
        def one(row, carry):
            at = pl.ds(pl.multiple_of(row * LANES, LANES), LANES)
            doc, image = id_row(row)
            q_docs[at, :] = jnp.broadcast_to(doc, (LANES, LANES)).T
            q_images[at, :] = jnp.broadcast_to(image, (LANES, LANES)).T
            return carry

        lax.fori_loop(0, BLOCK // LANES, one, 0)

    def make_bias(strip):
        start = first_key(strip)
        rows = pl.ds(pl.multiple_of(strip * STRIP, 64), STRIP)
        doc, image = q_docs[rows, :], q_images[rows, :]
        shape = (STRIP, LANES)
        offset = lax.broadcasted_iota(jnp.int32, shape, 1) - lax.broadcasted_iota(jnp.int32, shape, 0)
        first_row = lax.div(start, LANES) - FRONT // LANES
        for i in range(SPAN // LANES):
            key_doc, key_image = id_row(first_row + i)
            key_image = jnp.where(key_image < 0, -2, key_image)
            earlier = offset <= FRONT + strip * STRIP - start - i * LANES
            allowed = ((doc == key_doc) & earlier) | (image == key_image)
            bias[rows, i * LANES : (i + 1) * LANES] = jnp.where(allowed, 0.0, -jnp.inf)

    def attend(head, strip):
        start = first_key(strip)
        rows = pl.ds(pl.multiple_of(strip * STRIP, 64), STRIP)
        keys = pl.ds(start, SPAN)
        scores = lax.dot_general(
            q_buf[head, rows, :],
            k_buf[head, keys, :],
            (((1,), (1,)), ((), ())),
            preferred_element_type=jnp.float32,
        )
        scores = scores * (HEAD_DIM**-0.5 * math.log2(math.e)) + bias[rows, :]
        weights = jnp.exp2(scores - jnp.max(scores, axis=1, keepdims=True))
        total = jnp.sum(weights, axis=1, keepdims=True)
        mixed = jnp.dot(
            weights.astype(jnp.bfloat16), v_buf[head, keys, :], preferred_element_type=jnp.float32
        )
        o_buf[head, rows, :] = (mixed / total).astype(jnp.bfloat16)
        columns = pl.ds(pl.multiple_of(me * HEADS * HEAD_DIM + head * HEAD_DIM, LANES), HEAD_DIM)
        source, target = o_buf.at[head, rows, :], out_ref.at[:, columns]

        @pl.when(strip == me)
        def _():
            pltpu.make_async_copy(source, target, out_recv).start()

        @pl.when(strip != me)
        def _():
            pltpu.make_async_remote_copy(
                src_ref=source,
                dst_ref=target,
                send_sem=out_send,
                recv_sem=out_recv,
                device_id=member(strip),
                device_id_type=MESH,
            ).start()

    def first_groups(head, carry):
        start_group(0, head, first=head == 0)
        return carry

    stage_copies[0].wait()
    lax.fori_loop(0, HEADS - 1, first_groups, 0)
    lax.fori_loop(0, y, answer_lower, 0)
    tell(met_upper, has_lower, along_z(lower))
    tell(met_upper, has_lower & (y == 0), in_block(before))
    for copy in id_copies:
        copy.start()

    def clear(head, carry):
        def rows(first, count):
            for buffer in (k_buf, v_buf):
                buffer[head, first : first + count, :] = jnp.zeros((count, HEAD_DIM), jnp.bfloat16)

        rows(0, FRONT - BACK)
        rows(FRONT + BLOCK + AHEAD, WINDOW - FRONT - BLOCK - AHEAD)

        @pl.when(block == 0)
        def _():
            rows(FRONT - BACK, BACK)

        @pl.when(block == BLOCKS - 1)
        def _():
            rows(FRONT + BLOCK, AHEAD)

        return carry

    lax.fori_loop(0, HEADS, clear, 0)

    for array in range(2):

        def spread(head, carry, array=array):
            wait_group(array, head)
            if array == 0:

                @pl.when((head == 0) & (from_upper > 0))
                def _():
                    pl.semaphore_wait(met_upper, from_upper)

            start_halo(array, head)

            @pl.when(head == 0)
            def _():
                start_group(array, HEADS - 1)
                stage_copies[array + 1].wait()

            @pl.when(head > 0)
            def _():
                start_group(array + 1, head - 1)

            if array == 0:
                totals_start(head)
            else:
                relay_wait(head + 1)
                relay_start(head + 2)
            make_bias(array * HEADS + head)
            return carry

        lax.fori_loop(0, HEADS, spread, 0)

    def one_head(head, carry):
        for array in range(2):
            wait_halo(array, head)
        wait_group(2, head)

        @pl.when(head == 0)
        def _():
            start_group(2, HEADS - 1)

        def step(i, carry):
            j = i - 1
            steps = jnp.where(j < 2, 2, jnp.where(j < 6, 1 + (NX - 2) * lax.rem(j, 2), 0))
            other = jnp.where(j < 2, j, jnp.where(j < 6, lax.div(j - 2, 2), 1 - lax.rem(j, 2)))
            attend(head, toward(steps, other))
            return carry

        lax.fori_loop(1, GROUP + 1, step, 0)

        @pl.when(head == 0)
        def _():
            relay_wait(NZ - 3)
            relay_start(NZ - 2)

        @pl.when(head == 1)
        def _():
            relay_wait(NZ - 2)
            totals_end()

        @pl.when(head == 2)
        def _():
            for array in range(2):
                drain(targets[array].at[:, pl.ds(0, BLOCK - STRIP), :], in_send.at[array])
                drain_halo(array)
            for number, slots, size in ((0, slots_a, GROUP), (1, slots_b, NY)):
                drain(slots.at[pl.ds(0, size - 1)], stat_send.at[number])

            def relays_out(number, carry):
                relay_drain(number)
                return carry

            lax.fori_loop(0, NZ - 1, relays_out, 0)

        return carry

    lax.fori_loop(0, HEADS, one_head, 0)
    drain(q_buf.at[:, pl.ds(0, BLOCK - STRIP), :], in_send.at[2])
    drain(o_buf.at[:, pl.ds(0, BLOCK - STRIP), :], out_send)
    drain(out_ref, out_recv)


def store_kernel(chunks, attended, counts, losses, attended_out, counts_out, losses_out, sems):
    rows = attended.shape[0] // chunks
    parts = [(attended.at[pl.ds(i * rows, rows)], attended_out.at[pl.ds(i * rows, rows)]) for i in range(chunks)]
    parts += [(counts, counts_out), (losses, losses_out)]
    copies = [pltpu.make_async_copy(source, target, sems.at[i]) for i, (source, target) in enumerate(parts)]
    for copy in copies:
        copy.start()
    for copy in copies:
        copy.wait()


def store(attended, counts, losses, chunks=4):
    local = pl.BlockSpec(memory_space=pltpu.VMEM)
    anywhere = pl.BlockSpec(memory_space=pl.ANY)
    results = (attended, counts, losses)
    return pl.pallas_call(
        functools.partial(store_kernel, chunks),
        name="store_results",
        out_shape=tuple(jax.ShapeDtypeStruct(a.shape, a.dtype) for a in results),
        in_specs=[local] * 3,
        out_specs=(anywhere,) * 3,
        scratch_shapes=[pltpu.SemaphoreType.DMA((chunks + 2,))],
    )(*(pltpu.with_memory_space_constraint(a, pltpu.VMEM) for a in results))


def per_device(queries, key_rows, values, doc_ids, image_flags, labels, token_loss):
    documents = doc_ids.shape[0] // DOC_MEAN
    id_shape = (BLOCKS * BLOCK // LANES, LANES)
    anywhere = pl.BlockSpec(memory_space=pl.ANY)
    local = pl.BlockSpec(memory_space=pltpu.VMEM)
    window = pltpu.VMEM((HEADS, WINDOW, HEAD_DIM), jnp.bfloat16)
    own = pltpu.VMEM((HEADS, BLOCK, HEAD_DIM), jnp.bfloat16)
    attended, counts, losses = pl.pallas_call(
        kernel,
        name="exchange_and_attend",
        out_shape=(
            pltpu.VMEM(queries.shape, jnp.bfloat16),
            pltpu.VMEM((1, LANES), jnp.float32),
            pltpu.VMEM((1, LANES), jnp.float32),
        ),
        in_specs=[anywhere] * 7,
        out_specs=(local, local, local),
        scratch_shapes=[
            own,
            window,
            window,
            own,
            pltpu.VMEM((BLOCK, SPAN), jnp.float32),
            pltpu.VMEM(id_shape, jnp.int32),
            pltpu.VMEM(id_shape, jnp.int32),
            pltpu.VMEM((BLOCK, LANES), jnp.int32),
            pltpu.VMEM((BLOCK, LANES), jnp.int32),
            pltpu.VMEM((GROUP, 8, LANES), jnp.float32),
            pltpu.VMEM((NY, 8, LANES), jnp.float32),
            pltpu.VMEM((NZ, 8, LANES), jnp.float32),
            pltpu.VMEM((1, STRIP), jnp.int32),
            pltpu.VMEM((1, STRIP), jnp.float32),
            pltpu.VMEM((3,) + queries.shape, jnp.bfloat16),
            pltpu.SemaphoreType.DMA((3,)),
            pltpu.SemaphoreType.DMA((4,)),
            pltpu.SemaphoreType.DMA((3,)),
            pltpu.SemaphoreType.DMA((3, HEADS)),
            pltpu.SemaphoreType.DMA((2,)),
            pltpu.SemaphoreType.DMA((2, HEADS)),
            pltpu.SemaphoreType.DMA((2,)),
            pltpu.SemaphoreType.DMA((2, HEADS)),
            pltpu.SemaphoreType.DMA,
            pltpu.SemaphoreType.DMA,
            pltpu.SemaphoreType.DMA((2,)),
            pltpu.SemaphoreType.DMA((2,)),
            pltpu.SemaphoreType.DMA((2, NZ - 1)),
            pltpu.SemaphoreType.DMA((2, NZ - 1)),
            pltpu.SemaphoreType.REGULAR,
            pltpu.SemaphoreType.REGULAR,
        ],
        compiler_params=pltpu.CompilerParams(
            collective_id=0, has_side_effects=True, vmem_limit_bytes=40 * 1024 * 1024
        ),
    )(
        *(
            pltpu.with_memory_space_constraint(array, pltpu.HBM)
            for array in (
                queries,
                key_rows,
                values,
                doc_ids.reshape(id_shape),
                image_flags.reshape(id_shape),
                labels.reshape(1, STRIP),
                token_loss.reshape(1, STRIP),
            )
        )
    )
    attended, counts, losses = store(attended, counts, losses)
    return attended, counts.reshape(documents), losses.reshape(documents)


def solution(mesh):
    split = Mesh(mesh.devices.reshape(NZ, NY, NC, NX), AXES)
    return jax.shard_map(
        per_device,
        mesh=split,
        in_specs=(
            P(AXES, None),
            P(AXES, None),
            P(AXES, None),
            P(),
            P(),
            P(AXES),
            P(AXES),
        ),
        out_specs=(P(AXES, None), P(), P()),
        check_vma=False,
    )
```

```python
import functools
import math

import jax
import jax.numpy as jnp
from jax import lax
from jax.experimental import pallas as pl
from jax.experimental.pallas import tpu as pltpu
from jax.sharding import Mesh
from jax.sharding import PartitionSpec as P

HEAD_DIM = 128
DOC_MEAN = 384
NZ, NY, NC, NX = 8, 4, 2, 4
GROUP = NC * NX
STRIP = 192
BLOCK = STRIP * GROUP
BLOCKS = NZ * NY
HEADS = 4
BACK, AHEAD = 704, 576
FRONT = 768
SPAN = 1536
WINDOW = FRONT + BLOCK + 640
LANES = 128
AXES = ("z", "y", "c", "x")
MESH = pl.DeviceIdType.MESH


def first_key(strip):
    return pl.multiple_of(((3 * strip + 1) // 2) * LANES, LANES)


def kernel(
    q_hbm,
    k_hbm,
    v_hbm,
    docs_hbm,
    flags_hbm,
    labels_hbm,
    token_loss_hbm,
    out_ref,
    count_ref,
    loss_ref,
    q_buf,
    k_buf,
    v_buf,
    o_buf,
    bias,
    docs,
    flags,
    q_docs,
    q_images,
    slots_a,
    slots_b,
    slots_c,
    labels,
    token_loss,
    stage,
    stage_sem,
    id_sem,
    in_send,
    in_recv,
    back_send,
    back_recv,
    ahead_send,
    ahead_recv,
    out_send,
    out_recv,
    stat_send,
    stat_recv,
    relay_send,
    relay_recv,
    met_far,
    met_upper,
):
    z, y, c, x = (lax.axis_index(name) for name in AXES)
    me = c * NX + x
    block = z * NY + y
    has_after, has_before = block < BLOCKS - 1, block > 0
    after = lax.rem(block + 1, BLOCKS)
    before = lax.rem(block + BLOCKS - 1, BLOCKS)
    has_upper, has_lower = z < NZ - 1, z > 0
    upper, lower = lax.rem(z + 1, NZ), lax.rem(z + NZ - 1, NZ)

    def member(index):
        return {"z": z, "y": y, "c": lax.div(index, NX), "x": lax.rem(index, NX)}

    def in_block(index):
        return {"z": lax.div(index, NY), "y": lax.rem(index, NY), "c": c, "x": x}

    def along_y(index):
        return {"z": z, "y": index, "c": c, "x": x}

    def along_z(index):
        return {"z": index, "y": y, "c": c, "x": x}

    id_copies = [
        pltpu.make_async_copy(docs_hbm, docs, id_sem.at[0]),
        pltpu.make_async_copy(flags_hbm, flags, id_sem.at[1]),
        pltpu.make_async_copy(labels_hbm, labels, id_sem.at[2]),
        pltpu.make_async_copy(token_loss_hbm, token_loss, id_sem.at[3]),
    ]
    stage_copies = [
        pltpu.make_async_copy(source, stage.at[array], stage_sem.at[array])
        for array, source in enumerate((k_hbm, v_hbm, q_hbm))
    ]
    for copy in stage_copies:
        copy.start()

    barrier = pltpu.get_barrier_semaphore()
    def toward(steps, other):
        return lax.rem(c + other, NC) * NX + lax.rem(x + steps, NX)

    def tell(sem, present, peer):
        def signal():
            pl.semaphore_signal(sem, inc=1, device_id=peer, device_id_type=MESH)

        if present is None:
            signal()
        else:
            pl.when(present)(signal)

    def meet_near(o, carry):
        tell(barrier, None, member(toward(jnp.where(o == 4, 0, 1 + (NX - 2) * lax.rem(o, 2)), jnp.where(o < 2, 0, 1))))
        return carry

    def meet_higher(o, carry):
        tell(barrier, None, along_y(o))
        return carry

    def answer_lower(o, carry):
        tell(met_upper, None, along_y(o))
        return carry

    lax.fori_loop(0, 5, meet_near, 0)
    lax.fori_loop(y + 1, NY, meet_higher, 0)
    tell(barrier, has_upper, along_z(upper))
    tell(barrier, has_upper & (y == NY - 1), in_block(after))
    from_lower = jnp.where(has_lower, jnp.where(y == 0, 2, 1), 0) + y
    from_upper = jnp.where(has_upper, jnp.where(y == NY - 1, 2, 1), 0) + NY - 1 - y
    pl.semaphore_wait(barrier, 5 + from_lower)
    tell(met_far, None, member(toward(1, 0)))

    def drain(ref, sem):
        pltpu.make_async_copy(ref, ref, sem).wait()

    targets = (k_buf, v_buf, q_buf)
    bases = (FRONT, FRONT, 0)

    def piece(array, head, owner):
        columns = pl.ds(pl.multiple_of(owner * HEADS * HEAD_DIM + head * HEAD_DIM, LANES), HEAD_DIM)
        rows = pl.ds(pl.multiple_of(bases[array] + me * STRIP, 64), STRIP)
        return stage.at[array, :, columns], targets[array].at[head, rows, :]

    def start_group(array, head, first=None):
        def send(owner):
            source, target = piece(array, head, owner)
            pltpu.make_async_remote_copy(
                src_ref=source,
                dst_ref=target,
                send_sem=in_send.at[array],
                recv_sem=in_recv.at[array, head],
                device_id=member(owner),
                device_id_type=MESH,
            ).start()

        def near(o, carry):
            send(toward(1 + (NX - 2) * lax.rem(o + c, 2), lax.div(o, 2)))
            return carry

        def far(o, carry):
            send(toward(2, o))
            return carry

        lax.fori_loop(0, 2 * NC, near, 0)
        if first is not None:

            @pl.when(first)
            def _():
                pl.semaphore_wait(met_far, 1)

        lax.fori_loop(0, NC, far, 0)
        send(toward(0, 1))
        source, target = piece(array, head, me)
        pltpu.make_async_copy(source, target, in_recv.at[array, head]).start()

    def wait_group(array, head):
        rows = targets[array].at[head, pl.ds(bases[array], BLOCK), :]
        pltpu.make_async_copy(rows, rows, in_recv.at[array, head]).wait()

    def halos(array, head):
        return (
            (has_after, has_before, BACK, FRONT + BLOCK - BACK, FRONT - BACK, after, back_send, back_recv),
            (has_before, has_after, AHEAD, FRONT, FRONT + BLOCK, before, ahead_send, ahead_recv),
        )

    def start_halo(array, head):
        buffer = targets[array]
        for sends, _, rows, first, target, peer, send_sem, recv_sem in halos(array, head):

            @pl.when(sends)
            def _():
                pltpu.make_async_remote_copy(
                    src_ref=buffer.at[head, pl.ds(first, rows), :],
                    dst_ref=buffer.at[head, pl.ds(target, rows), :],
                    send_sem=send_sem.at[array],
                    recv_sem=recv_sem.at[array, head],
                    device_id=in_block(peer),
                    device_id_type=MESH,
                ).start()

    def wait_halo(array, head):
        for _, receives, rows, _, target, _, _, recv_sem in halos(array, head):

            @pl.when(receives)
            def _():
                drain(targets[array].at[head, pl.ds(target, rows), :], recv_sem.at[array, head])

    def drain_halo(array):
        for sends, _, rows, _, _, _, send_sem, _ in halos(array, 0):

            @pl.when(sends)
            def _():
                drain(targets[array].at[:, pl.ds(0, rows), :], send_sem.at[array])

    def stage_send(number, slots, own, size, peer_of):
        def send(o, carry):
            pltpu.make_async_remote_copy(
                src_ref=slots.at[own],
                dst_ref=slots.at[own],
                send_sem=stat_send.at[number],
                recv_sem=stat_recv.at[number],
                device_id=peer_of(lax.rem(own + o, size)),
                device_id_type=MESH,
            ).start()
            return carry

        lax.fori_loop(1, size, send, 0)

    def stage_sum(number, slots, size):
        others = slots.at[pl.ds(0, size - 1)]
        pltpu.make_async_copy(others, others, stat_recv.at[number]).wait()
        total = slots[0]
        for i in range(1, size):
            total = total + slots[i]
        return total

    def relays(step):
        return (
            (has_upper & (z >= step), z - step, has_lower & (z >= step + 1), z - 1 - step, upper, 0),
            (has_lower & (z + step < NZ), z + step, has_upper & (z + step + 1 < NZ), z + 1 + step, lower, 1),
        )

    def relay_copy(step, slot, peer, way):
        return pltpu.make_async_remote_copy(
            src_ref=slots_c.at[slot],
            dst_ref=slots_c.at[slot],
            send_sem=relay_send.at[way, step],
            recv_sem=relay_recv.at[way, step],
            device_id=along_z(peer),
            device_id_type=MESH,
        )

    def relay_start(step):
        for sends, slot, _, _, peer, way in relays(step):

            @pl.when(sends)
            def _():
                relay_copy(step, slot, peer, way).start()

    def relay_wait(step):
        for _, _, receives, slot, peer, way in relays(step):

            @pl.when(receives)
            def _():
                drain(slots_c.at[slot], relay_recv.at[way, step])

    def relay_drain(step):
        for sends, slot, _, _, peer, way in relays(step):

            @pl.when(sends)
            def _():
                drain(slots_c.at[slot], relay_send.at[way, step])

    def document_partials():
        first = lax.div(block * BLOCK + me * STRIP, LANES)
        pair = jnp.concatenate([docs[pl.ds(first, 1), :], docs[pl.ds(first + 1, 1), :]], axis=1)
        half = jnp.concatenate([pair[:, 64:], pair[:, :64]], axis=1)
        doc = jnp.where(lax.rem(me, 2) == 1, half, pair)[:, :STRIP]
        weight = jnp.where(labels[...] >= 0, 1.0, 0.0)
        lines = lax.broadcasted_iota(jnp.int32, (8, STRIP), 0)
        terms = jnp.where(lines == 0, weight, jnp.where(lines == 1, weight * token_loss[...], 0.0))
        hit = jnp.where(lax.broadcasted_iota(jnp.int32, (LANES, STRIP), 0) == doc, 1.0, 0.0)
        return lax.dot_general(
            terms,
            hit,
            (((1,), (1,)), ((), ())),
            precision=lax.Precision.HIGHEST,
            preferred_element_type=jnp.float32,
        )

    def totals_start(head):
        @pl.when(head == 0)
        def _():
            for copy in id_copies:
                copy.wait()
            slots_a[me] = document_partials()
            stage_send(0, slots_a, me, GROUP, member)
            make_query_ids()

        @pl.when(head == 1)
        def _():
            slots_b[y] = stage_sum(0, slots_a, GROUP)
            stage_send(1, slots_b, y, NY, along_y)

        @pl.when(head == 2)
        def _():
            slots_c[z] = stage_sum(1, slots_b, NY)
            relay_start(0)

        @pl.when(head == 3)
        def _():
            relay_wait(0)
            relay_start(1)

    def totals_end():
        total = slots_c[0]
        for i in range(1, NZ):
            total = total + slots_c[i]
        counts = total[0:1]
        count_ref[...] = counts
        loss_ref[...] = total[1:2] / jnp.maximum(counts, 1.0)

    def id_row(row):
        at = pl.ds(lax.rem(block * (BLOCK // LANES) + row + BLOCKS * (BLOCK // LANES), BLOCKS * (BLOCK // LANES)), 1)
        doc = docs[at, :]
        return doc, jnp.where(flags[at, :] == 1, doc, -1)

    def make_query_ids():
        def one(row, carry):
            at = pl.ds(pl.multiple_of(row * LANES, LANES), LANES)
            doc, image = id_row(row)
            q_docs[at, :] = jnp.broadcast_to(doc, (LANES, LANES)).T
            q_images[at, :] = jnp.broadcast_to(image, (LANES, LANES)).T
            return carry

        lax.fori_loop(0, BLOCK // LANES, one, 0)

    def make_bias(strip):
        start = first_key(strip)
        rows = pl.ds(pl.multiple_of(strip * STRIP, 64), STRIP)
        doc, image = q_docs[rows, :], q_images[rows, :]
        shape = (STRIP, LANES)
        offset = lax.broadcasted_iota(jnp.int32, shape, 1) - lax.broadcasted_iota(jnp.int32, shape, 0)
        first_row = lax.div(start, LANES) - FRONT // LANES
        for i in range(SPAN // LANES):
            key_doc, key_image = id_row(first_row + i)
            key_image = jnp.where(key_image < 0, -2, key_image)
            earlier = offset <= FRONT + strip * STRIP - start - i * LANES
            allowed = ((doc == key_doc) & earlier) | (image == key_image)
            bias[rows, i * LANES : (i + 1) * LANES] = jnp.where(allowed, 0.0, -jnp.inf)

    def attend(head, strip):
        start = first_key(strip)
        rows = pl.ds(pl.multiple_of(strip * STRIP, 64), STRIP)
        keys = pl.ds(start, SPAN)
        scores = lax.dot_general(
            q_buf[head, rows, :],
            k_buf[head, keys, :],
            (((1,), (1,)), ((), ())),
            preferred_element_type=jnp.float32,
        )
        scores = scores * (HEAD_DIM**-0.5 * math.log2(math.e)) + bias[rows, :]
        weights = jnp.exp2(scores - jnp.max(scores, axis=1, keepdims=True))
        total = jnp.sum(weights, axis=1, keepdims=True)
        mixed = jnp.dot(
            weights.astype(jnp.bfloat16), v_buf[head, keys, :], preferred_element_type=jnp.float32
        )
        o_buf[head, rows, :] = (mixed / total).astype(jnp.bfloat16)
        columns = pl.ds(pl.multiple_of(me * HEADS * HEAD_DIM + head * HEAD_DIM, LANES), HEAD_DIM)
        source, target = o_buf.at[head, rows, :], out_ref.at[:, columns]

        @pl.when(strip == me)
        def _():
            pltpu.make_async_copy(source, target, out_recv).start()

        @pl.when(strip != me)
        def _():
            pltpu.make_async_remote_copy(
                src_ref=source,
                dst_ref=target,
                send_sem=out_send,
                recv_sem=out_recv,
                device_id=member(strip),
                device_id_type=MESH,
            ).start()

    def first_groups(head, carry):
        start_group(0, head, first=head == 0)
        return carry

    stage_copies[0].wait()
    lax.fori_loop(0, HEADS - 1, first_groups, 0)
    lax.fori_loop(0, y, answer_lower, 0)
    tell(met_upper, has_lower, along_z(lower))
    tell(met_upper, has_lower & (y == 0), in_block(before))
    for copy in id_copies:
        copy.start()

    def clear(head, carry):
        def rows(first, count):
            for buffer in (k_buf, v_buf):
                buffer[head, first : first + count, :] = jnp.zeros((count, HEAD_DIM), jnp.bfloat16)

        rows(0, FRONT - BACK)
        rows(FRONT + BLOCK + AHEAD, WINDOW - FRONT - BLOCK - AHEAD)

        @pl.when(block == 0)
        def _():
            rows(FRONT - BACK, BACK)

        @pl.when(block == BLOCKS - 1)
        def _():
            rows(FRONT + BLOCK, AHEAD)

        return carry

    lax.fori_loop(0, HEADS, clear, 0)

    for array in range(2):

        def spread(head, carry, array=array):
            wait_group(array, head)
            if array == 0:

                @pl.when((head == 0) & (from_upper > 0))
                def _():
                    pl.semaphore_wait(met_upper, from_upper)

            start_halo(array, head)

            @pl.when(head == 0)
            def _():
                start_group(array, HEADS - 1)
                stage_copies[array + 1].wait()

            @pl.when(head > 0)
            def _():
                start_group(array + 1, head - 1)

            if array == 0:
                totals_start(head)
            else:
                relay_wait(head + 1)
                relay_start(head + 2)
            make_bias(array * HEADS + head)
            return carry

        lax.fori_loop(0, HEADS, spread, 0)

    def one_head(head, carry):
        for array in range(2):
            wait_halo(array, head)
        wait_group(2, head)

        @pl.when(head == 0)
        def _():
            start_group(2, HEADS - 1)

        def step(i, carry):
            j = i - 1
            steps = jnp.where(j < 2, 2, jnp.where(j < 6, 1 + (NX - 2) * lax.rem(j + c, 2), 0))
            other = jnp.where(j < 2, j, jnp.where(j < 6, lax.div(j - 2, 2), 1 - lax.rem(j, 2)))
            attend(head, toward(steps, other))
            return carry

        lax.fori_loop(1, GROUP + 1, step, 0)

        @pl.when(head == 0)
        def _():
            relay_wait(NZ - 3)
            relay_start(NZ - 2)

        @pl.when(head == 1)
        def _():
            relay_wait(NZ - 2)
            totals_end()

        @pl.when(head == 2)
        def _():
            for array in range(2):
                drain(targets[array].at[:, pl.ds(0, BLOCK - STRIP), :], in_send.at[array])
                drain_halo(array)
            for number, slots, size in ((0, slots_a, GROUP), (1, slots_b, NY)):
                drain(slots.at[pl.ds(0, size - 1)], stat_send.at[number])

            def relays_out(number, carry):
                relay_drain(number)
                return carry

            lax.fori_loop(0, NZ - 1, relays_out, 0)

        return carry

    lax.fori_loop(0, HEADS, one_head, 0)
    drain(q_buf.at[:, pl.ds(0, BLOCK - STRIP), :], in_send.at[2])
    drain(o_buf.at[:, pl.ds(0, BLOCK - STRIP), :], out_send)
    drain(out_ref, out_recv)


def store_kernel(chunks, attended, counts, losses, attended_out, counts_out, losses_out, sems):
    rows = attended.shape[0] // chunks
    parts = [(attended.at[pl.ds(i * rows, rows)], attended_out.at[pl.ds(i * rows, rows)]) for i in range(chunks)]
    parts += [(counts, counts_out), (losses, losses_out)]
    copies = [pltpu.make_async_copy(source, target, sems.at[i]) for i, (source, target) in enumerate(parts)]
    for copy in copies:
        copy.start()
    for copy in copies:
        copy.wait()


def store(attended, counts, losses, chunks=4):
    local = pl.BlockSpec(memory_space=pltpu.VMEM)
    anywhere = pl.BlockSpec(memory_space=pl.ANY)
    results = (attended, counts, losses)
    return pl.pallas_call(
        functools.partial(store_kernel, chunks),
        name="store_results",
        out_shape=tuple(jax.ShapeDtypeStruct(a.shape, a.dtype) for a in results),
        in_specs=[local] * 3,
        out_specs=(anywhere,) * 3,
        scratch_shapes=[pltpu.SemaphoreType.DMA((chunks + 2,))],
    )(*(pltpu.with_memory_space_constraint(a, pltpu.VMEM) for a in results))


def per_device(queries, key_rows, values, doc_ids, image_flags, labels, token_loss):
    documents = doc_ids.shape[0] // DOC_MEAN
    id_shape = (BLOCKS * BLOCK // LANES, LANES)
    anywhere = pl.BlockSpec(memory_space=pl.ANY)
    local = pl.BlockSpec(memory_space=pltpu.VMEM)
    window = pltpu.VMEM((HEADS, WINDOW, HEAD_DIM), jnp.bfloat16)
    own = pltpu.VMEM((HEADS, BLOCK, HEAD_DIM), jnp.bfloat16)
    attended, counts, losses = pl.pallas_call(
        kernel,
        name="exchange_and_attend",
        out_shape=(
            pltpu.VMEM(queries.shape, jnp.bfloat16),
            pltpu.VMEM((1, LANES), jnp.float32),
            pltpu.VMEM((1, LANES), jnp.float32),
        ),
        in_specs=[anywhere] * 7,
        out_specs=(local, local, local),
        scratch_shapes=[
            own,
            window,
            window,
            own,
            pltpu.VMEM((BLOCK, SPAN), jnp.float32),
            pltpu.VMEM(id_shape, jnp.int32),
            pltpu.VMEM(id_shape, jnp.int32),
            pltpu.VMEM((BLOCK, LANES), jnp.int32),
            pltpu.VMEM((BLOCK, LANES), jnp.int32),
            pltpu.VMEM((GROUP, 8, LANES), jnp.float32),
            pltpu.VMEM((NY, 8, LANES), jnp.float32),
            pltpu.VMEM((NZ, 8, LANES), jnp.float32),
            pltpu.VMEM((1, STRIP), jnp.int32),
            pltpu.VMEM((1, STRIP), jnp.float32),
            pltpu.VMEM((3,) + queries.shape, jnp.bfloat16),
            pltpu.SemaphoreType.DMA((3,)),
            pltpu.SemaphoreType.DMA((4,)),
            pltpu.SemaphoreType.DMA((3,)),
            pltpu.SemaphoreType.DMA((3, HEADS)),
            pltpu.SemaphoreType.DMA((2,)),
            pltpu.SemaphoreType.DMA((2, HEADS)),
            pltpu.SemaphoreType.DMA((2,)),
            pltpu.SemaphoreType.DMA((2, HEADS)),
            pltpu.SemaphoreType.DMA,
            pltpu.SemaphoreType.DMA,
            pltpu.SemaphoreType.DMA((2,)),
            pltpu.SemaphoreType.DMA((2,)),
            pltpu.SemaphoreType.DMA((2, NZ - 1)),
            pltpu.SemaphoreType.DMA((2, NZ - 1)),
            pltpu.SemaphoreType.REGULAR,
            pltpu.SemaphoreType.REGULAR,
        ],
        compiler_params=pltpu.CompilerParams(
            collective_id=0, has_side_effects=True, vmem_limit_bytes=40 * 1024 * 1024
        ),
    )(
        *(
            pltpu.with_memory_space_constraint(array, pltpu.HBM)
            for array in (
                queries,
                key_rows,
                values,
                doc_ids.reshape(id_shape),
                image_flags.reshape(id_shape),
                labels.reshape(1, STRIP),
                token_loss.reshape(1, STRIP),
            )
        )
    )
    attended, counts, losses = store(attended, counts, losses)
    return attended, counts.reshape(documents), losses.reshape(documents)


def solution(mesh):
    split = Mesh(mesh.devices.reshape(NZ, NY, NC, NX), AXES)
    return jax.shard_map(
        per_device,
        mesh=split,
        in_specs=(
            P(AXES, None),
            P(AXES, None),
            P(AXES, None),
            P(),
            P(),
            P(AXES),
            P(AXES),
        ),
        out_specs=(P(AXES, None), P(), P()),
        check_vma=False,
    )
```

```python
import functools
import math

import jax
import jax.numpy as jnp
from jax import lax
from jax.experimental import pallas as pl
from jax.experimental.pallas import tpu as pltpu
from jax.sharding import Mesh
from jax.sharding import PartitionSpec as P

HEAD_DIM = 128
DOC_MEAN = 384
NZ, NY, NC, NX = 8, 4, 2, 4
GROUP = NC * NX
STRIP = 192
BLOCK = STRIP * GROUP
BLOCKS = NZ * NY
HEADS = 4
BACK, AHEAD = 704, 576
FRONT = 768
SPAN = 1536
WINDOW = FRONT + BLOCK + 640
LANES = 128
AXES = ("z", "y", "c", "x")
MESH = pl.DeviceIdType.MESH


def first_key(strip):
    return pl.multiple_of(((3 * strip + 1) // 2) * LANES, LANES)


def kernel(
    q_hbm,
    k_hbm,
    v_hbm,
    docs_hbm,
    flags_hbm,
    labels_hbm,
    token_loss_hbm,
    out_ref,
    count_ref,
    loss_ref,
    q_buf,
    k_buf,
    v_buf,
    o_buf,
    bias,
    docs,
    flags,
    q_docs,
    q_images,
    slots_a,
    slots_b,
    slots_c,
    labels,
    token_loss,
    stage,
    stage_sem,
    id_sem,
    in_send,
    in_recv,
    back_send,
    back_recv,
    ahead_send,
    ahead_recv,
    out_send,
    out_recv,
    stat_send,
    stat_recv,
    relay_send,
    relay_recv,
    met_far,
    met_upper,
):
    z, y, c, x = (lax.axis_index(name) for name in AXES)
    me = c * NX + x
    block = z * NY + y
    has_after, has_before = block < BLOCKS - 1, block > 0
    after = lax.rem(block + 1, BLOCKS)
    before = lax.rem(block + BLOCKS - 1, BLOCKS)
    has_upper, has_lower = z < NZ - 1, z > 0
    upper, lower = lax.rem(z + 1, NZ), lax.rem(z + NZ - 1, NZ)

    def member(index):
        return {"z": z, "y": y, "c": lax.div(index, NX), "x": lax.rem(index, NX)}

    def in_block(index):
        return {"z": lax.div(index, NY), "y": lax.rem(index, NY), "c": c, "x": x}

    def along_y(index):
        return {"z": z, "y": index, "c": c, "x": x}

    def along_z(index):
        return {"z": index, "y": y, "c": c, "x": x}

    id_copies = [
        pltpu.make_async_copy(docs_hbm, docs, id_sem.at[0]),
        pltpu.make_async_copy(flags_hbm, flags, id_sem.at[1]),
        pltpu.make_async_copy(labels_hbm, labels, id_sem.at[2]),
        pltpu.make_async_copy(token_loss_hbm, token_loss, id_sem.at[3]),
    ]
    stage_copies = [
        pltpu.make_async_copy(source, stage.at[array], stage_sem.at[array])
        for array, source in enumerate((k_hbm, v_hbm, q_hbm))
    ]
    for copy in stage_copies:
        copy.start()

    barrier = pltpu.get_barrier_semaphore()
    def toward(steps, other):
        return lax.rem(c + other, NC) * NX + lax.rem(x + steps, NX)

    def tell(sem, present, peer):
        def signal():
            pl.semaphore_signal(sem, inc=1, device_id=peer, device_id_type=MESH)

        if present is None:
            signal()
        else:
            pl.when(present)(signal)

    def meet_near(o, carry):
        tell(barrier, None, member(toward(jnp.where(o == 4, 0, 1 + (NX - 2) * lax.rem(o, 2)), jnp.where(o < 2, 0, 1))))
        return carry

    def meet_higher(o, carry):
        tell(barrier, None, along_y(o))
        return carry

    def answer_lower(o, carry):
        tell(met_upper, None, along_y(o))
        return carry

    lax.fori_loop(0, 5, meet_near, 0)
    lax.fori_loop(y + 1, NY, meet_higher, 0)
    tell(barrier, has_upper, along_z(upper))
    tell(barrier, has_upper & (y == NY - 1), in_block(after))
    from_lower = jnp.where(has_lower, jnp.where(y == 0, 2, 1), 0) + y
    from_upper = jnp.where(has_upper, jnp.where(y == NY - 1, 2, 1), 0) + NY - 1 - y
    pl.semaphore_wait(barrier, 5 + from_lower)
    tell(met_far, None, member(toward(1, 0)))

    def drain(ref, sem):
        pltpu.make_async_copy(ref, ref, sem).wait()

    targets = (k_buf, v_buf, q_buf)
    bases = (FRONT, FRONT, 0)

    def piece(array, head, owner):
        columns = pl.ds(pl.multiple_of(owner * HEADS * HEAD_DIM + head * HEAD_DIM, LANES), HEAD_DIM)
        rows = pl.ds(pl.multiple_of(bases[array] + me * STRIP, 64), STRIP)
        return stage.at[array, :, columns], targets[array].at[head, rows, :]

    def start_group(array, head, first=None):
        def send(owner):
            source, target = piece(array, head, owner)
            pltpu.make_async_remote_copy(
                src_ref=source,
                dst_ref=target,
                send_sem=in_send.at[array],
                recv_sem=in_recv.at[array, head],
                device_id=member(owner),
                device_id_type=MESH,
            ).start()

        def near(o, carry):
            send(toward(1 + (NX - 2) * lax.rem(o, 2), lax.div(o, 2)))
            return carry

        def far(o, carry):
            send(toward(2, o))
            return carry

        lax.fori_loop(0, 2 * NC, near, 0)
        if first is not None:

            @pl.when(first)
            def _():
                pl.semaphore_wait(met_far, 1)

        lax.fori_loop(0, NC, far, 0)
        send(toward(0, 1))
        source, target = piece(array, head, me)
        pltpu.make_async_copy(source, target, in_recv.at[array, head]).start()

    def wait_group(array, head):
        rows = targets[array].at[head, pl.ds(bases[array], BLOCK), :]
        pltpu.make_async_copy(rows, rows, in_recv.at[array, head]).wait()

    def halos(array, head):
        return (
            (has_after, has_before, BACK, FRONT + BLOCK - BACK, FRONT - BACK, after, back_send, back_recv),
            (has_before, has_after, AHEAD, FRONT, FRONT + BLOCK, before, ahead_send, ahead_recv),
        )

    def start_halo(array, head):
        buffer = targets[array]
        for sends, _, rows, first, target, peer, send_sem, recv_sem in halos(array, head):

            @pl.when(sends)
            def _():
                pltpu.make_async_remote_copy(
                    src_ref=buffer.at[head, pl.ds(first, rows), :],
                    dst_ref=buffer.at[head, pl.ds(target, rows), :],
                    send_sem=send_sem.at[array],
                    recv_sem=recv_sem.at[array, head],
                    device_id=in_block(peer),
                    device_id_type=MESH,
                ).start()

    def wait_halo(array, head):
        for _, receives, rows, _, target, _, _, recv_sem in halos(array, head):

            @pl.when(receives)
            def _():
                drain(targets[array].at[head, pl.ds(target, rows), :], recv_sem.at[array, head])

    def drain_halo(array):
        for sends, _, rows, _, _, _, send_sem, _ in halos(array, 0):

            @pl.when(sends)
            def _():
                drain(targets[array].at[:, pl.ds(0, rows), :], send_sem.at[array])

    def stage_send(number, slots, own, size, peer_of):
        def send(o, carry):
            pltpu.make_async_remote_copy(
                src_ref=slots.at[own],
                dst_ref=slots.at[own],
                send_sem=stat_send.at[number],
                recv_sem=stat_recv.at[number],
                device_id=peer_of(lax.rem(own + o, size)),
                device_id_type=MESH,
            ).start()
            return carry

        lax.fori_loop(1, size, send, 0)

    def stage_sum(number, slots, size):
        others = slots.at[pl.ds(0, size - 1)]
        pltpu.make_async_copy(others, others, stat_recv.at[number]).wait()
        total = slots[0]
        for i in range(1, size):
            total = total + slots[i]
        return total

    def relays(step):
        return (
            (has_upper & (z >= step), z - step, has_lower & (z >= step + 1), z - 1 - step, upper, 0),
            (has_lower & (z + step < NZ), z + step, has_upper & (z + step + 1 < NZ), z + 1 + step, lower, 1),
        )

    def relay_copy(step, slot, peer, way):
        return pltpu.make_async_remote_copy(
            src_ref=slots_c.at[slot],
            dst_ref=slots_c.at[slot],
            send_sem=relay_send.at[way, step],
            recv_sem=relay_recv.at[way, step],
            device_id=along_z(peer),
            device_id_type=MESH,
        )

    def relay_start(step):
        for sends, slot, _, _, peer, way in relays(step):

            @pl.when(sends)
            def _():
                relay_copy(step, slot, peer, way).start()

    def relay_wait(step):
        for _, _, receives, slot, peer, way in relays(step):

            @pl.when(receives)
            def _():
                drain(slots_c.at[slot], relay_recv.at[way, step])

    def relay_drain(step):
        for sends, slot, _, _, peer, way in relays(step):

            @pl.when(sends)
            def _():
                drain(slots_c.at[slot], relay_send.at[way, step])

    def document_partials():
        first = lax.div(block * BLOCK + me * STRIP, LANES)
        pair = jnp.concatenate([docs[pl.ds(first, 1), :], docs[pl.ds(first + 1, 1), :]], axis=1)
        half = jnp.concatenate([pair[:, 64:], pair[:, :64]], axis=1)
        doc = jnp.where(lax.rem(me, 2) == 1, half, pair)[:, :STRIP]
        weight = jnp.where(labels[...] >= 0, 1.0, 0.0)
        lines = lax.broadcasted_iota(jnp.int32, (8, STRIP), 0)
        terms = jnp.where(lines == 0, weight, jnp.where(lines == 1, weight * token_loss[...], 0.0))
        hit = jnp.where(lax.broadcasted_iota(jnp.int32, (LANES, STRIP), 0) == doc, 1.0, 0.0)
        return lax.dot_general(
            terms,
            hit,
            (((1,), (1,)), ((), ())),
            precision=lax.Precision.HIGHEST,
            preferred_element_type=jnp.float32,
        )

    def totals_start(head):
        @pl.when(head == 0)
        def _():
            for copy in id_copies:
                copy.wait()
            slots_a[me] = document_partials()
            stage_send(0, slots_a, me, GROUP, member)
            make_query_ids()

        @pl.when(head == 1)
        def _():
            slots_b[y] = stage_sum(0, slots_a, GROUP)
            stage_send(1, slots_b, y, NY, along_y)

        @pl.when(head == 2)
        def _():
            slots_c[z] = stage_sum(1, slots_b, NY)
            relay_start(0)

        @pl.when(head == 3)
        def _():
            relay_wait(0)
            relay_start(1)

    def totals_end():
        total = slots_c[0]
        for i in range(1, NZ):
            total = total + slots_c[i]
        counts = total[0:1]
        count_ref[...] = counts
        loss_ref[...] = total[1:2] / jnp.maximum(counts, 1.0)

    def id_row(row):
        at = pl.ds(lax.rem(block * (BLOCK // LANES) + row + BLOCKS * (BLOCK // LANES), BLOCKS * (BLOCK // LANES)), 1)
        doc = docs[at, :]
        return doc, jnp.where(flags[at, :] == 1, doc, -1)

    def make_query_ids():
        def one(row, carry):
            at = pl.ds(pl.multiple_of(row * LANES, LANES), LANES)
            doc, image = id_row(row)
            q_docs[at, :] = jnp.broadcast_to(doc, (LANES, LANES)).T
            q_images[at, :] = jnp.broadcast_to(image, (LANES, LANES)).T
            return carry

        lax.fori_loop(0, BLOCK // LANES, one, 0)

    def make_bias(strip):
        start = first_key(strip)
        rows = pl.ds(pl.multiple_of(strip * STRIP, 64), STRIP)
        doc, image = q_docs[rows, :], q_images[rows, :]
        shape = (STRIP, LANES)
        offset = lax.broadcasted_iota(jnp.int32, shape, 1) - lax.broadcasted_iota(jnp.int32, shape, 0)
        first_row = lax.div(start, LANES) - FRONT // LANES
        for i in range(SPAN // LANES):
            key_doc, key_image = id_row(first_row + i)
            key_image = jnp.where(key_image < 0, -2, key_image)
            earlier = offset <= FRONT + strip * STRIP - start - i * LANES
            allowed = ((doc == key_doc) & earlier) | (image == key_image)
            bias[rows, i * LANES : (i + 1) * LANES] = jnp.where(allowed, 0.0, -jnp.inf)

    def attend(head, strip):
        start = first_key(strip)
        rows = pl.ds(pl.multiple_of(strip * STRIP, 64), STRIP)
        keys = pl.ds(start, SPAN)
        scores = lax.dot_general(
            q_buf[head, rows, :],
            k_buf[head, keys, :],
            (((1,), (1,)), ((), ())),
            preferred_element_type=jnp.float32,
        )
        scores = scores * (HEAD_DIM**-0.5 * math.log2(math.e)) + bias[rows, :]
        weights = jnp.exp2(scores - jnp.max(scores, axis=1, keepdims=True))
        total = jnp.sum(weights, axis=1, keepdims=True)
        mixed = jnp.dot(
            weights.astype(jnp.bfloat16), v_buf[head, keys, :], preferred_element_type=jnp.float32
        )
        o_buf[head, rows, :] = (mixed / total).astype(jnp.bfloat16)
        columns = pl.ds(pl.multiple_of(me * HEADS * HEAD_DIM + head * HEAD_DIM, LANES), HEAD_DIM)
        source, target = o_buf.at[head, rows, :], out_ref.at[:, columns]

        @pl.when(strip == me)
        def _():
            pltpu.make_async_copy(source, target, out_recv).start()

        @pl.when(strip != me)
        def _():
            pltpu.make_async_remote_copy(
                src_ref=source,
                dst_ref=target,
                send_sem=out_send,
                recv_sem=out_recv,
                device_id=member(strip),
                device_id_type=MESH,
            ).start()

    def first_groups(head, carry):
        start_group(0, head, first=head == 0)
        return carry

    stage_copies[0].wait()
    lax.fori_loop(0, HEADS - 1, first_groups, 0)
    lax.fori_loop(0, y, answer_lower, 0)
    tell(met_upper, has_lower, along_z(lower))
    tell(met_upper, has_lower & (y == 0), in_block(before))
    for copy in id_copies:
        copy.start()

    def clear(head, carry):
        def rows(first, count):
            for buffer in (k_buf, v_buf):
                buffer[head, first : first + count, :] = jnp.zeros((count, HEAD_DIM), jnp.bfloat16)

        rows(0, FRONT - BACK)
        rows(FRONT + BLOCK + AHEAD, WINDOW - FRONT - BLOCK - AHEAD)

        @pl.when(block == 0)
        def _():
            rows(FRONT - BACK, BACK)

        @pl.when(block == BLOCKS - 1)
        def _():
            rows(FRONT + BLOCK, AHEAD)

        return carry

    lax.fori_loop(0, HEADS, clear, 0)

    for array in range(2):

        def spread(head, carry, array=array):
            wait_group(array, head)
            @pl.when(head == 0)
            def _():
                start_group(array, HEADS - 1)
                stage_copies[array + 1].wait()

            @pl.when(head > 0)
            def _():
                start_group(array + 1, head - 1)

            if array == 0:

                @pl.when((head == 0) & (from_upper > 0))
                def _():
                    pl.semaphore_wait(met_upper, from_upper)

            start_halo(array, head)

            if array == 0:
                totals_start(head)
            else:
                relay_wait(head + 1)
                relay_start(head + 2)
            make_bias(array * HEADS + head)
            return carry

        lax.fori_loop(0, HEADS, spread, 0)

    def one_head(head, carry):
        for array in range(2):
            wait_halo(array, head)
        wait_group(2, head)

        @pl.when(head == 0)
        def _():
            start_group(2, HEADS - 1)

        def step(i, carry):
            j = i - 1
            steps = jnp.where(j < 2, 2, jnp.where(j < 6, 1 + (NX - 2) * lax.rem(j, 2), 0))
            other = jnp.where(j < 2, j, jnp.where(j < 6, lax.div(j - 2, 2), 1 - lax.rem(j, 2)))
            attend(head, toward(steps, other))
            return carry

        lax.fori_loop(1, GROUP + 1, step, 0)

        @pl.when(head == 0)
        def _():
            relay_wait(NZ - 3)
            relay_start(NZ - 2)

        @pl.when(head == 1)
        def _():
            relay_wait(NZ - 2)
            totals_end()

        @pl.when(head == 2)
        def _():
            for array in range(2):
                drain(targets[array].at[:, pl.ds(0, BLOCK - STRIP), :], in_send.at[array])
                drain_halo(array)
            for number, slots, size in ((0, slots_a, GROUP), (1, slots_b, NY)):
                drain(slots.at[pl.ds(0, size - 1)], stat_send.at[number])

            def relays_out(number, carry):
                relay_drain(number)
                return carry

            lax.fori_loop(0, NZ - 1, relays_out, 0)

        return carry

    lax.fori_loop(0, HEADS, one_head, 0)
    drain(q_buf.at[:, pl.ds(0, BLOCK - STRIP), :], in_send.at[2])
    drain(o_buf.at[:, pl.ds(0, BLOCK - STRIP), :], out_send)
    drain(out_ref, out_recv)


def store_kernel(chunks, attended, counts, losses, attended_out, counts_out, losses_out, sems):
    rows = attended.shape[0] // chunks
    parts = [(attended.at[pl.ds(i * rows, rows)], attended_out.at[pl.ds(i * rows, rows)]) for i in range(chunks)]
    parts += [(counts, counts_out), (losses, losses_out)]
    copies = [pltpu.make_async_copy(source, target, sems.at[i]) for i, (source, target) in enumerate(parts)]
    for copy in copies:
        copy.start()
    for copy in copies:
        copy.wait()


def store(attended, counts, losses, chunks=4):
    local = pl.BlockSpec(memory_space=pltpu.VMEM)
    anywhere = pl.BlockSpec(memory_space=pl.ANY)
    results = (attended, counts, losses)
    return pl.pallas_call(
        functools.partial(store_kernel, chunks),
        name="store_results",
        out_shape=tuple(jax.ShapeDtypeStruct(a.shape, a.dtype) for a in results),
        in_specs=[local] * 3,
        out_specs=(anywhere,) * 3,
        scratch_shapes=[pltpu.SemaphoreType.DMA((chunks + 2,))],
    )(*(pltpu.with_memory_space_constraint(a, pltpu.VMEM) for a in results))


def per_device(queries, key_rows, values, doc_ids, image_flags, labels, token_loss):
    documents = doc_ids.shape[0] // DOC_MEAN
    id_shape = (BLOCKS * BLOCK // LANES, LANES)
    anywhere = pl.BlockSpec(memory_space=pl.ANY)
    local = pl.BlockSpec(memory_space=pltpu.VMEM)
    window = pltpu.VMEM((HEADS, WINDOW, HEAD_DIM), jnp.bfloat16)
    own = pltpu.VMEM((HEADS, BLOCK, HEAD_DIM), jnp.bfloat16)
    attended, counts, losses = pl.pallas_call(
        kernel,
        name="exchange_and_attend",
        out_shape=(
            pltpu.VMEM(queries.shape, jnp.bfloat16),
            pltpu.VMEM((1, LANES), jnp.float32),
            pltpu.VMEM((1, LANES), jnp.float32),
        ),
        in_specs=[anywhere] * 7,
        out_specs=(local, local, local),
        scratch_shapes=[
            own,
            window,
            window,
            own,
            pltpu.VMEM((BLOCK, SPAN), jnp.float32),
            pltpu.VMEM(id_shape, jnp.int32),
            pltpu.VMEM(id_shape, jnp.int32),
            pltpu.VMEM((BLOCK, LANES), jnp.int32),
            pltpu.VMEM((BLOCK, LANES), jnp.int32),
            pltpu.VMEM((GROUP, 8, LANES), jnp.float32),
            pltpu.VMEM((NY, 8, LANES), jnp.float32),
            pltpu.VMEM((NZ, 8, LANES), jnp.float32),
            pltpu.VMEM((1, STRIP), jnp.int32),
            pltpu.VMEM((1, STRIP), jnp.float32),
            pltpu.VMEM((3,) + queries.shape, jnp.bfloat16),
            pltpu.SemaphoreType.DMA((3,)),
            pltpu.SemaphoreType.DMA((4,)),
            pltpu.SemaphoreType.DMA((3,)),
            pltpu.SemaphoreType.DMA((3, HEADS)),
            pltpu.SemaphoreType.DMA((2,)),
            pltpu.SemaphoreType.DMA((2, HEADS)),
            pltpu.SemaphoreType.DMA((2,)),
            pltpu.SemaphoreType.DMA((2, HEADS)),
            pltpu.SemaphoreType.DMA,
            pltpu.SemaphoreType.DMA,
            pltpu.SemaphoreType.DMA((2,)),
            pltpu.SemaphoreType.DMA((2,)),
            pltpu.SemaphoreType.DMA((2, NZ - 1)),
            pltpu.SemaphoreType.DMA((2, NZ - 1)),
            pltpu.SemaphoreType.REGULAR,
            pltpu.SemaphoreType.REGULAR,
        ],
        compiler_params=pltpu.CompilerParams(
            collective_id=0, has_side_effects=True, vmem_limit_bytes=40 * 1024 * 1024
        ),
    )(
        *(
            pltpu.with_memory_space_constraint(array, pltpu.HBM)
            for array in (
                queries,
                key_rows,
                values,
                doc_ids.reshape(id_shape),
                image_flags.reshape(id_shape),
                labels.reshape(1, STRIP),
                token_loss.reshape(1, STRIP),
            )
        )
    )
    attended, counts, losses = store(attended, counts, losses)
    return attended, counts.reshape(documents), losses.reshape(documents)


def solution(mesh):
    split = Mesh(mesh.devices.reshape(NZ, NY, NC, NX), AXES)
    return jax.shard_map(
        per_device,
        mesh=split,
        in_specs=(
            P(AXES, None),
            P(AXES, None),
            P(AXES, None),
            P(),
            P(),
            P(AXES),
            P(AXES),
        ),
        out_specs=(P(AXES, None), P(), P()),
        check_vma=False,
    )
```
